32 devices in a mesh: group: 2 (over y), tile: 4 (over z), col: 2 (over x), layer: 2 (over core).
Axes of the slice: x: 2, y: 2, z: 4, core: 2. Of those that a mesh axis runs over, the one named last changes fastest.
Arguments:
- source: float32 [4, 40, 96, 512], P('group', 'layer', 'tile', 'col'), parts along dimension 0, may hold values from -12 to 12
- profile: float32 [40], P('layer'), may hold values from 0.5 to 1
- column: float32 [192, 512], P(('group', 'tile'), 'col'), parts along dimension 0, may hold values from 0.6 to 1.2
- terrain_height_error: int32 [4, 96, 512], P('group', 'tile', 'col'), parts along dimension 0, may hold values from -150 to 149
Outputs:
- solution: float32 [4, 40, 96, 512], P('group', 'layer', 'tile', 'col'), parts along dimension 0
The draws below stay inside these ranges and needn't reach their ends.
There are 2 independent parts, one for each index of `group`. The reference program is written for one: setup_inputs(seed, part) draws one part's arguments, and reference() takes and returns one part's arrays. A program takes and returns all parts, laid end to end along the dimension named above; an argument that names none is the same for every part. Nothing has to cross between parts.
All inputs are finite; a program needn't handle non-finite values.
Results may differ from the reference program's by a relative error of at most 0.0001.
Values sent between devices are 32-bit elements; how exact they have to be, the bound alone decides.
No kernel may reach another device: no remote copies, remote signals or barrier semaphores. Data moves between devices by JAX's collectives and lax.ppermute only.
A program may use at most 64 MiB of HBM per device.

```python
import math
import jax
import jax.numpy as jnp

NZ = 40
ITERS = 2
CELLS_FIRST = 96
CELLS_SECOND = 512


def draw_source(key, part):
    key_base = jax.random.fold_in(key, 11)
    shape = (2, NZ, CELLS_FIRST, CELLS_SECOND)
    place = jnp.arange(CELLS_FIRST, dtype=jnp.float32) / jnp.float32(max(CELLS_FIRST - 1, 1))
    ramp = (1.0 + 2.0 * place)[None, None, :, None]
    base = jnp.clip(jax.random.normal(key_base, shape, jnp.float32), -4.0, 4.0)
    value = base * ramp
    return jnp.clip(value, -12.0, 12.0)


def place_ends(result, rng, low, largest):
    longest = result.shape.index(max(result.shape))
    spots = []
    for shift in (0, 1):
        where = [jax.random.randint(jax.random.fold_in(rng, axis), (), 0, length) for axis, length in enumerate(result.shape)]
        where[longest] = (where[longest] + shift) % result.shape[longest]
        spots.append(tuple(where))
    return result.at[spots[0]].set(low).at[spots[1]].set(largest)


def block_levels(stream_key, dims, cuts, low, largest):
    level = 1.0
    for position, blocks in cuts:
        draws = jax.random.uniform(jax.random.fold_in(jax.random.fold_in(stream_key, 6), position), (blocks,), jnp.float32, low / len(cuts), largest / len(cuts))
        level = level * jnp.repeat(jnp.exp(draws), dims[position] // blocks).reshape((-1,) + (1,) * (len(dims) - 1 - position))
    return level


def setup_inputs(seed: int = 0, part: int = 0) -> dict:
    streams_of = jax.random.split(jax.random.key(seed), 5)
    part_keys = jax.random.split(jax.random.fold_in(streams_of[4], part), 5)
    source = draw_source(jax.random.fold_in(jax.random.fold_in(streams_of[4], part), 71), part)
    profile = jnp.clip(jnp.exp(math.log(1.0) - 0.6931472 * jax.random.uniform(streams_of[1], (NZ,), jnp.float32) ** block_levels(streams_of[1], (NZ,), ((0, 2),), -0.2, 0.2)), 0.5, 1.0)
    column = jnp.clip(jnp.exp(math.log(1.2) - 0.6931472 * jax.random.uniform(part_keys[2], (CELLS_FIRST, CELLS_SECOND), jnp.float32) ** block_levels(part_keys[2], (CELLS_FIRST, CELLS_SECOND), ((0, 4), (1, 2)), -0.2, 0.2)), 0.6, 1.2)
    terrain_height_error = place_ends(jax.random.randint(part_keys[3], (2, CELLS_FIRST, CELLS_SECOND), -150, 150), jax.random.fold_in(part_keys[3], 1), -150, 149).astype(jnp.int32)
    return {"source": source, "profile": profile, "column": column, "terrain_height_error": terrain_height_error}


weight_horiz = 1.0
weight_vert = 2.0
weight_cross = 0.3
gain_bound = 1.6
total_weight = 10.4
diag_shift = 0.5
source_scale = 8.0


def stencil_sum(padded):
    horiz = padded[:, 1:-1, 2:, 1:-1] + padded[:, 1:-1, :-2, 1:-1] + padded[:, 1:-1, 1:-1, 2:] + padded[:, 1:-1, 1:-1, :-2]
    vert = padded[:, 2:, 1:-1, 1:-1] + padded[:, :-2, 1:-1, 1:-1]
    cross = padded[:, 2:, 2:, 1:-1] + padded[:, 2:, :-2, 1:-1] + padded[:, :-2, 2:, 1:-1] + padded[:, :-2, :-2, 1:-1]
    cross = cross + padded[:, 2:, 1:-1, 2:] + padded[:, 2:, 1:-1, :-2] + padded[:, :-2, 1:-1, 2:] + padded[:, :-2, 1:-1, :-2]
    return weight_horiz * horiz + weight_vert * vert + weight_cross * cross


def apply_operator(field, metric, diag_full):
    padded = jnp.pad(metric * field, ((0, 0), (1, 1), (1, 1), (1, 1)))
    return diag_full * field - metric * stencil_sum(padded)


def error_spread(values):
    return values[:, None, None, None]


def reference(source, profile, column, terrain_height_error):
    multiplier_factor = 1.0 + 0.002 * terrain_height_error.astype(jnp.float32)
    metric = profile[None, :, None, None] * column[None, None, :, :] * multiplier_factor[:, None, :, :]
    diag_full = gain_bound * total_weight * metric + diag_shift
    forcing_term = source_scale * metric * source
    residual = forcing_term
    scaled = forcing_term / diag_full
    applied = apply_operator(scaled, metric, diag_full)
    solution = jnp.zeros_like(forcing_term)
    direction = jnp.zeros_like(forcing_term)
    search_img = jnp.zeros_like(forcing_term)
    preconditioned_direction = jnp.zeros_like(forcing_term)
    img_dir = jnp.zeros_like(forcing_term)
    gamma_old = None
    alpha_old = None
    for step in range(ITERS):
        gamma_now = jnp.sum(residual * scaled, axis=(1, 2, 3))
        delta_now = jnp.sum(applied * scaled, axis=(1, 2, 3))
        pre_app = applied / diag_full
        preconditioned_image = apply_operator(pre_app, metric, diag_full)
        if step == 0:
            beta_now = jnp.zeros_like(gamma_now)
            alpha_now = gamma_now / delta_now
        else:
            beta_now = gamma_now / gamma_old
            alpha_now = gamma_now / (delta_now - beta_now * gamma_now / alpha_old)
        img_dir = preconditioned_image + error_spread(beta_now) * img_dir
        preconditioned_direction = pre_app + error_spread(beta_now) * preconditioned_direction
        search_img = applied + error_spread(beta_now) * search_img
        direction = scaled + error_spread(beta_now) * direction
        solution = solution + error_spread(alpha_now) * direction
        residual = residual - error_spread(alpha_now) * search_img
        scaled = scaled - error_spread(alpha_now) * preconditioned_direction
        applied = applied - error_spread(alpha_now) * img_dir
        gamma_old = gamma_now
        alpha_old = alpha_now
    return solution
```

```python
import jax
import jax.numpy as jnp
from jax import lax
from jax.sharding import PartitionSpec as P

weight_vert = 2.0
weight_cross = 0.3
gain_bound = 1.6
total_weight = 10.4
diag_shift = 0.5
source_scale = 8.0


def line_pairs(count, first):
    pairs = []
    for low in range(first, count - 1, 2):
        pairs += [(low, low + 1), (low + 1, low)]
    return pairs


def neighbours(low_edge, high_edge, axis):
    count, index = lax.axis_size(axis), lax.axis_index(axis)
    if count == 1:
        return jnp.zeros_like(low_edge), jnp.zeros_like(high_edge)
    even = index % 2 == 0
    first = lax.ppermute(jnp.where(even, high_edge, low_edge), axis, line_pairs(count, 0))
    if count == 2:
        second = jnp.zeros_like(first)
    else:
        second = lax.ppermute(jnp.where(even, low_edge, high_edge), axis, line_pairs(count, 1))
    return jnp.where(even, second, first), jnp.where(even, first, second)


def padded(shard, axis, dim):
    length = shard.shape[dim]
    before, after = neighbours(
        lax.slice_in_dim(shard, 0, 1, axis=dim), lax.slice_in_dim(shard, length - 1, length, axis=dim), axis
    )
    return jnp.concatenate([before, shard, after], axis=dim)


def stencil(field):
    field = padded(padded(padded(field, "layer", 1), "tile", 2), "col", 3)
    sides = (
        field[:, :, 2:, 1:-1] + field[:, :, :-2, 1:-1] + field[:, :, 1:-1, 2:] + field[:, :, 1:-1, :-2]
    )
    levels = weight_vert * field[:, :, 1:-1, 1:-1] + weight_cross * sides
    return sides[:, 1:-1] + levels[:, 2:] + levels[:, :-2]


def total(values, axes):
    for axis in axes:
        count = lax.axis_size(axis)
        if count & (count - 1):
            values = lax.psum(values, axis)
            continue
        bit = 1
        while bit < count:
            values = values + lax.ppermute(values, axis, [(i, i ^ bit) for i in range(count)])
            bit *= 2
    return values


def local(source, profile, column, terrain_height_error):
    multiplier_factor = 1.0 + 0.002 * terrain_height_error.astype(jnp.float32)
    metric = profile[None, :, None, None] * column[None, None, :, :] * multiplier_factor[:, None, :, :]
    scale = metric / (gain_bound * total_weight * metric + diag_shift)
    gain = metric * scale
    forcing = source_scale * source
    weighted = gain * forcing
    image = stencil(weighted)
    again = gain * image
    image_again = stencil(again)
    lanes = (1, 2)
    sums = jnp.stack(
        [
            jnp.sum(weighted * forcing, axis=lanes),
            jnp.sum(weighted * image, axis=lanes),
            jnp.sum(again * image, axis=lanes),
            jnp.sum(again * image_again, axis=lanes),
        ]
    )
    sums = jnp.sum(total(sums, ("layer", "col", "tile")), axis=-1)
    zz, zb, bb, bbb = (sums[i][:, None, None, None] for i in range(4))
    delta = zz - zb
    alpha = zz / delta
    rest = -zb / delta
    beta = (zz * bb - zb * zb) / (delta * delta)
    gamma = zz * beta
    delta_next = gamma - (rest * rest * zb + 2.0 * alpha * rest * bb + alpha * alpha * bbb)
    alpha_next = gamma / (delta_next - beta * gamma / alpha)
    return scale * ((alpha + alpha_next * (rest + beta)) * forcing + (alpha_next * alpha) * image)


def solution(mesh):
    placed = (
        P("group", "layer", "tile", "col"),
        P("layer"),
        P(("group", "tile"), "col"),
        P("group", "tile", "col"),
    )
    return jax.shard_map(
        local,
        mesh=mesh,
        in_specs=placed,
        out_specs=P("group", "layer", "tile", "col"),
        check_vma=False,
    )
```

```python
import functools

import jax
import jax.numpy as jnp
from jax import lax
from jax.experimental import pallas as pl
from jax.experimental.pallas import tpu as pltpu
from jax.sharding import PartitionSpec as P

weight_vert = 2.0
weight_cross = 0.3
gain_bound = 1.6
total_weight = 10.4
diag_shift = 0.5
source_scale = 8.0

LANES = 128
GRANT = 8 << 20


def line_pairs(count, first):
    pairs = []
    for low in range(first, count - 1, 2):
        pairs += [(low, low + 1), (low + 1, low)]
    return pairs


def neighbours(low_edge, high_edge, axis):
    count, index = lax.axis_size(axis), lax.axis_index(axis)
    if count == 1:
        return jnp.zeros_like(low_edge), jnp.zeros_like(high_edge)
    even = index % 2 == 0
    first = lax.ppermute(jnp.where(even, high_edge, low_edge), axis, line_pairs(count, 0))
    if count == 2:
        second = jnp.zeros_like(first)
    else:
        second = lax.ppermute(jnp.where(even, low_edge, high_edge), axis, line_pairs(count, 1))
    return jnp.where(even, second, first), jnp.where(even, first, second)


def flipped(values, sizes, axes, bits):
    shape = [sizes[axis] for axis in axes]
    pairs = []
    for flat in range(functools.reduce(lambda a, b: a * b, shape, 1)):
        place, rest = [], flat
        for size in reversed(shape):
            place.insert(0, rest % size)
            rest //= size
        target = 0
        for where, size, bit in zip(place, shape, bits):
            target = target * size + (where ^ bit)
        pairs.append((flat, target))
    return lax.ppermute(values, axes, pairs)


def total(values):
    sizes = {axis: lax.axis_size(axis) for axis in ("layer", "col", "tile")}
    assert all(size & (size - 1) == 0 for size in sizes.values())
    first = 1
    if sizes["col"] > 1 and sizes["layer"] == 2:
        values = (
            values
            + flipped(values, sizes, ("layer",), (1,))
            + flipped(values, sizes, ("col",), (1,))
            + flipped(values, sizes, ("col", "layer"), (1, 1))
        )
        first = 2
    else:
        values = values + flipped(values, sizes, ("layer",), (1,))
    for axis, bit in (("col", first), ("tile", 1)):
        while bit < sizes[axis]:
            values = values + flipped(values, sizes, (axis,), (bit,))
            bit *= 2
    return values


def tiles_of(plane):
    return [plane[:, at : at + LANES] for at in range(0, plane.shape[1], LANES)]


def sides(tiles, low_row, high_row, low_col, high_col):
    rows, lanes = tiles[0].shape
    row = lax.broadcasted_iota(jnp.int32, (rows, lanes), 0)
    lane = lax.broadcasted_iota(jnp.int32, (rows, lanes), 1)
    ahead = [pltpu.roll(tile, lanes - 1, 1) for tile in tiles]
    behind = [pltpu.roll(tile, 1, 1) for tile in tiles]
    ahead.append(0.0 if high_col is None else high_col)
    behind.insert(0, 0.0 if low_col is None else low_col)
    out = []
    for i, tile in enumerate(tiles):
        below = jnp.where(row == rows - 1, 0.0 if high_row is None else high_row[i], pltpu.roll(tile, rows - 1, 0))
        above = jnp.where(row == 0, 0.0 if low_row is None else low_row[i], pltpu.roll(tile, 1, 0))
        right = jnp.where(lane == lanes - 1, ahead[i + 1], ahead[i])
        left = jnp.where(lane == 0, behind[i], behind[i + 1])
        out.append((below + above) + (right + left))
    return out


def levels(tiles, side):
    return [weight_vert * tile + weight_cross * s for tile, s in zip(tiles, side)]


def gains(level, column, multiplier):
    metric = level * column * multiplier
    scale = metric / (gain_bound * total_weight * metric + diag_shift)
    return metric, scale


def edges_out(k, tiles, rows_low, rows_high, packs):
    rows, lanes = tiles[0].shape
    for i, tile in enumerate(tiles):
        at = i * (rows_low.shape[0] // len(tiles)) + k
        rows_low[pl.ds(at, 1), :] = tile[0:1]
        rows_high[pl.ds(at, 1), :] = tile[rows - 1 : rows]
    lane = lax.broadcasted_iota(jnp.int32, (rows, lanes), 1)
    low, high = packs
    low = jnp.where(lane == k, pltpu.roll(tiles[0], k, 1), low)
    high = jnp.where(lane == k, pltpu.roll(tiles[-1], k + 1, 1), high)
    return low, high


def weighted_kernel(
    own, other, profile_own, profile_other, column, error, weighted, gain, rows_low, rows_high, cols_low, cols_high, sums
):
    layer = lax.axis_index("layer")
    half, rows, width = own.shape[1:]
    columns = column[...]
    multiplier = 1.0 + 0.002 * error[layer].astype(jnp.float32)

    def part(source, profile, base, carry):
        def step(at, carry):
            packs, acc = carry
            k = base + at
            metric, scale = gains(profile[at], columns, multiplier)
            g = metric * scale
            forcing = source_scale * source[layer, at]
            u = g * forcing
            weighted[k] = u
            gain[k] = g
            packs = edges_out(k, tiles_of(u), rows_low, rows_high, packs)
            return packs, acc + u * forcing

        return lax.fori_loop(0, half, step, carry, unroll=4)

    zeros = jnp.zeros((rows, LANES), jnp.float32)
    carry = ((zeros, zeros), jnp.zeros((rows, width), jnp.float32))
    carry = part(own, profile_own, layer * half, carry)
    (low, high), acc = part(other, profile_other, (1 - layer) * half, carry)
    cols_low[...] = low
    cols_high[...] = high
    sums[...] = acc


def image_kernel(
    weighted,
    gain,
    low_rows,
    high_rows,
    low_cols,
    high_cols,
    kept,
    sent,
    again,
    rows_low,
    rows_high,
    cols_low,
    cols_high,
    sums,
):
    layer = lax.axis_index("layer")
    count, rows, width = weighted.shape
    half = count // 2
    base = layer * half
    starts = [i * count for i in range(width // LANES)]
    pack_low, pack_high = low_cols[...], high_cols[...]

    def emit(k, u, image, packs, acc):
        both = jnp.concatenate(image, axis=1)
        ub = gain[k] * both
        again[k] = ub
        inside = (k >= base) & (k < base + half)

        @pl.when(inside)
        def _():
            kept[k - base] = both

        @pl.when(jnp.logical_not(inside))
        def _():
            sent[k - (half - base)] = both

        packs = edges_out(k, tiles_of(ub), rows_low, rows_high, packs)
        return packs, (acc[0] + u * both, acc[1] + ub * both)

    def step(k, carry):
        side_before, level_twice, level_before, packs, acc = carry
        tiles = tiles_of(weighted[k])
        low_row = [low_rows[pl.ds(start + k, 1), :] for start in starts]
        high_row = [high_rows[pl.ds(start + k, 1), :] for start in starts]
        low_col = pltpu.roll(pack_low, lax.rem(LANES - k, LANES), 1)
        high_col = pltpu.roll(pack_high, LANES - 1 - k, 1)
        side = sides(tiles, low_row, high_row, low_col, high_col)
        level = levels(tiles, side)
        image = [s + a + b for s, a, b in zip(side_before, level_twice, level)]
        before = jnp.maximum(k - 1, 0)
        packs, acc = emit(before, weighted[before], image, packs, acc)
        return side, level_before, level, packs, acc

    zero = [jnp.zeros((rows, LANES), jnp.float32) for _ in starts]
    pack = jnp.zeros((rows, LANES), jnp.float32)
    full = jnp.zeros((rows, width), jnp.float32)
    first_tiles = tiles_of(weighted[0])
    first = sides(
        first_tiles,
        [low_rows[start : start + 1, :] for start in starts],
        [high_rows[start : start + 1, :] for start in starts],
        pack_low,
        pltpu.roll(pack_high, LANES - 1, 1),
    )
    carry = (first, zero, levels(first_tiles, first), (pack, pack), (full, full))
    side, level_twice, _, packs, acc = lax.fori_loop(1, count, step, carry, unroll=3)
    image = [s + a for s, a in zip(side, level_twice)]
    packs, acc = emit(count - 1, weighted[count - 1], image, packs, acc)
    cols_low[...], cols_high[...] = packs
    sums[0], sums[1] = acc


def quadratic_kernel(again, sums):
    count, rows, width = again.shape

    def step(k, carry):
        before, acc = carry
        plane = again[k]
        tiles = tiles_of(plane)
        side = sides(tiles, None, None, None, None)
        level = jnp.concatenate(levels(tiles, side), axis=1)
        acc = acc + plane * jnp.concatenate(side, axis=1) + 2.0 * before * level
        return plane, acc

    zero = jnp.zeros((rows, width), jnp.float32)
    _, acc = lax.fori_loop(0, count, step, (zero, zero), unroll=4)
    sums[...] = acc


def near(values, axis, count):
    size = values.shape[axis]
    place = lax.rem(lax.broadcasted_iota(jnp.int32, values.shape, axis), count)
    up = jnp.where(place == count - 1, 0.0, pltpu.roll(values, size - 1, axis))
    down = jnp.where(place == 0, 0.0, pltpu.roll(values, 1, axis))
    return values + weight_cross * (up + down)


def collect_kernel(
    rows_low, rows_high, cols_low, cols_high, low_rows, high_rows, low_cols, high_cols, sum_a, sum_b, sum_c, out
):
    layer = lax.axis_index("layer")
    count = rows_low.shape[0] // (sum_a.shape[1] // LANES)
    cross_rows = rows_low[...] * near(low_rows[...], 0, count) + rows_high[...] * near(high_rows[...], 0, count)
    cross_cols = cols_low[...] * near(low_cols[...], 1, LANES) + cols_high[...] * near(high_cols[...], 1, LANES)

    def line(values):
        values = jnp.sum(values, axis=0, keepdims=True)
        return functools.reduce(lambda a, b: a + b, tiles_of(values))

    out[...] = jnp.zeros_like(out)
    out[pl.ds(8 * layer, 1), :] = line(sum_a[...])
    out[pl.ds(8 * layer + 1, 1), :] = line(sum_b[0])
    out[pl.ds(8 * layer + 2, 1), :] = line(sum_b[1])
    out[pl.ds(8 * layer + 3, 1), :] = line(sum_c[...]) + line(cross_rows) + line(cross_cols)


def final_kernel(source, profile, column, error, kept, other, sums, out):
    layer = lax.axis_index("layer")
    half = source.shape[1]
    columns = column[...]

    def factors(base):
        values = jnp.sum(sums[pl.ds(base, 8), :], axis=1, keepdims=True)
        zz, zb, bb, bbb = (values[i : i + 1] for i in range(4))
        delta = zz - zb
        alpha = zz / delta
        rest = -zb / delta
        beta = (zz * bb - zb * zb) / (delta * delta)
        gamma = zz * beta
        delta_next = gamma - (rest * rest * zb + 2.0 * alpha * rest * bb + alpha * alpha * bbb)
        alpha_next = gamma / (delta_next - beta * gamma / alpha)
        return source_scale * (alpha + alpha_next * (rest + beta)), alpha_next * alpha

    for which, image in ((layer, kept), (1 - layer, other)):
        multiplier = 1.0 + 0.002 * error[which].astype(jnp.float32)
        first, second = factors(8 * which)

        def step(k, _):
            _, scale = gains(profile[k], columns, multiplier)
            out[which, k] = scale * (first * source[which, k] + second * image[k])
            return 0

        lax.fori_loop(0, half, step, 0, unroll=4)


def call(kernel, out_shape, args, name, scalars=()):
    vmem = pl.BlockSpec(memory_space=pltpu.VMEM)
    smem = pl.BlockSpec(memory_space=pltpu.SMEM)
    return pl.pallas_call(
        kernel,
        out_shape=[jax.ShapeDtypeStruct(shape, jnp.float32) for shape in out_shape],
        in_specs=[smem if i in scalars else vmem for i in range(len(args))],
        out_specs=[vmem] * len(out_shape),
        compiler_params=pltpu.CompilerParams(vmem_limit_bytes=GRANT),
        name=name,
    )(*args)


def local(source, profile, column, terrain_height_error):
    copies, half, rows, width = source.shape
    count = 2 * half
    assert lax.axis_size("layer") == copies == 2 and count <= LANES and width % LANES == 0
    swap = [(0, 1), (1, 0)]
    other = lax.ppermute(source, "layer", swap)
    profile_other = lax.ppermute(profile, "layer", swap)
    block, row, pack = (count, rows, width), (width // LANES * count, LANES), (rows, LANES)
    weighted, gain, rows_low, rows_high, cols_low, cols_high, sum_a = call(
        weighted_kernel,
        [block, block, row, row, pack, pack, (rows, width)],
        (source, other, profile, profile_other, column, terrain_height_error),
        "weighted",
        (2, 3),
    )
    low_rows, high_rows = neighbours(rows_low, rows_high, "tile")
    low_cols, high_cols = neighbours(cols_low, cols_high, "col")
    part = (half, rows, width)
    kept, sent, again, rows_low, rows_high, cols_low, cols_high, sum_b = call(
        image_kernel,
        [part, part, block, row, row, pack, pack, (2, rows, width)],
        (weighted, gain, low_rows, high_rows, low_cols, high_cols),
        "image",
    )
    low_rows, high_rows = neighbours(rows_low, rows_high, "tile")
    low_cols, high_cols = neighbours(cols_low, cols_high, "col")
    received = lax.ppermute(sent, "layer", swap)
    (sum_c,) = call(quadratic_kernel, [(rows, width)], (again,), "quadratic")
    (sums,) = call(
        collect_kernel,
        [(16, LANES)],
        (rows_low, rows_high, cols_low, cols_high, low_rows, high_rows, low_cols, high_cols, sum_a, sum_b, sum_c),
        "collect",
    )
    sums = total(sums)
    (out,) = call(
        final_kernel,
        [source.shape],
        (source, profile, column, terrain_height_error, kept, received, sums),
        "final",
        (1,),
    )
    return out


def solution(mesh):
    placed = (
        P("group", "layer", "tile", "col"),
        P("layer"),
        P(("group", "tile"), "col"),
        P("group", "tile", "col"),
    )
    return jax.shard_map(
        local,
        mesh=mesh,
        in_specs=placed,
        out_specs=P("group", "layer", "tile", "col"),
        check_vma=False,
    )
```

```python
import functools

import jax
import jax.numpy as jnp
from jax import lax
from jax.experimental import pallas as pl
from jax.experimental.pallas import tpu as pltpu
from jax.sharding import PartitionSpec as P

weight_vert = 2.0
weight_cross = 0.3
gain_bound = 1.6
total_weight = 10.4
diag_shift = 0.5
source_scale = 8.0

LANES = 128
GRANT = 8 << 20


def line_pairs(count, first):
    pairs = []
    for low in range(first, count - 1, 2):
        pairs += [(low, low + 1), (low + 1, low)]
    return pairs


def exchanged(for_pairs, for_others, axis):
    count = lax.axis_size(axis)
    if count == 1:
        return jnp.zeros_like(for_pairs), jnp.zeros_like(for_others)
    first = lax.ppermute(for_pairs, axis, line_pairs(count, 0))
    if count == 2:
        return first, jnp.zeros_like(first)
    return first, lax.ppermute(for_others, axis, line_pairs(count, 1))


def flipped(values, sizes, axes, bits):
    shape = [sizes[axis] for axis in axes]
    pairs = []
    for flat in range(functools.reduce(lambda a, b: a * b, shape, 1)):
        place, rest = [], flat
        for size in reversed(shape):
            place.insert(0, rest % size)
            rest //= size
        target = 0
        for where, size, bit in zip(place, shape, bits):
            target = target * size + (where ^ bit)
        pairs.append((flat, target))
    return lax.ppermute(values, axes, pairs)


def total(values):
    sizes = {axis: lax.axis_size(axis) for axis in ("layer", "col", "tile")}
    assert all(size & (size - 1) == 0 for size in sizes.values())
    first = 1
    if sizes["col"] > 1 and sizes["layer"] == 2:
        values = (
            values
            + flipped(values, sizes, ("layer",), (1,))
            + flipped(values, sizes, ("col",), (1,))
            + flipped(values, sizes, ("col", "layer"), (1, 1))
        )
        first = 2
    else:
        values = values + flipped(values, sizes, ("layer",), (1,))
    for axis, bit in (("col", first), ("tile", 1)):
        while bit < sizes[axis]:
            values = values + flipped(values, sizes, (axis,), (bit,))
            bit *= 2
    return values


def tiles_of(plane):
    return [plane[:, at : at + LANES] for at in range(0, plane.shape[1], LANES)]


def iota(shape, axis):
    return lax.broadcasted_iota(jnp.int32, shape, axis)


def turned(values, by, axis):
    by %= values.shape[axis]
    return pltpu.roll(values, by, axis) if by else values


def sides(tiles, low_col, high_col):
    rows, lanes = tiles[0].shape
    row, lane = iota((rows, lanes), 0), iota((rows, lanes), 1)
    ahead = [turned(tile, -1, 1) for tile in tiles] + [0.0 if high_col is None else high_col]
    behind = [0.0 if low_col is None else low_col] + [turned(tile, 1, 1) for tile in tiles]
    out = []
    for i, tile in enumerate(tiles):
        below = jnp.where(row == rows - 1, 0.0, turned(tile, -1, 0))
        above = jnp.where(row == 0, 0.0, turned(tile, 1, 0))
        right = jnp.where(lane == lanes - 1, ahead[i + 1], ahead[i])
        left = jnp.where(lane == 0, behind[i], behind[i + 1])
        out.append((below + above) + (right + left))
    return out


def levels(tiles, side):
    return [weight_vert * tile + weight_cross * s for tile, s in zip(tiles, side)]


def gains(metric):
    scale = metric / (gain_bound * total_weight * metric + diag_shift)
    return metric * scale, scale


def folded(values):
    return functools.reduce(lambda a, b: a + b, [values[at : at + 8] for at in range(0, values.shape[0], 8)])


def dot(left, right):
    return functools.reduce(lambda a, b: a + b, [folded(a * b) for a, b in zip(left, right)])


def keep_rows(k, tiles, low, high, count):
    rows = tiles[0].shape[0]
    for i, tile in enumerate(tiles):
        if low is not None:
            low[pl.ds(i * count + k, 1), :] = tile[0:1]
        if high is not None:
            high[pl.ds(i * count + k, 1), :] = tile[rows - 1 : rows]


def multiplier_of(error, which):
    return 1.0 + 0.002 * error[which].astype(jnp.float32)


def weighted_kernel(own, *refs):
    source, profile, column, error = refs[:4]
    weighted, gain, strip_low, strip_high, cols_low, cols_high, prof, sums = refs[-8:]
    layer = lax.axis_index("layer")
    half, rows, width = source.shape[1:]
    count, tiles = 2 * half, width // LANES
    base = layer * half if own else (1 - layer) * half
    columns = column[...] * multiplier_of(error, layer)
    lane = iota((rows, LANES), 1)

    def step(at, carry):
        first, second, last, acc = carry
        k = base + at
        g, _ = gains(profile[at] * columns)
        forcing = source_scale * source[layer, at]
        u = g * forcing
        weighted[k] = u
        gain[k] = g
        parts = tiles_of(u)
        keep_rows(k, parts, strip_low, strip_high, count)
        for i, part in enumerate(parts):
            strip_low[pl.ds((tiles + i) * count + k, 1), :] = part[1:2]
        prof[pl.ds(k, 1), :] = jnp.full((1, LANES), profile[at])
        first = jnp.where(lane == k, pltpu.roll(parts[0], k, 1), first)
        second = jnp.where(lane == k, pltpu.roll(parts[0], lax.rem(k + LANES - 1, LANES), 1), second)
        last = jnp.where(lane == k, pltpu.roll(parts[-1], k + 1, 1), last)
        return first, second, last, acc + dot(parts, tiles_of(forcing))

    if own:
        zeros = jnp.zeros((rows, LANES), jnp.float32)
        edge = tiles_of(columns)
        carry = (jnp.where(lane == LANES - 1, turned(edge[0], -1, 1), 0.0), zeros, zeros, jnp.zeros((8, LANES), jnp.float32))
        for i, tile in enumerate(edge):
            strip_low[2 * tiles * count + 2 + i : 2 * tiles * count + 3 + i, :] = tile[0:1]
    else:
        low, high, acc = refs[8], refs[9], refs[11]
        carry = (low[0:rows], low[rows:], high[0:rows], acc[...])
    first, second, last, acc = lax.fori_loop(0, half, step, carry, unroll=4)
    cols_low[0:rows] = first
    cols_low[rows:] = second
    cols_high[0:rows] = last
    cols_high[rows:] = jnp.zeros_like(last)
    sums[...] = acc


def join_kernel(nr, strip_low, strip_high, pair_cols, other_cols, for_pairs, for_others):
    rows = pair_cols.shape[0] // 2
    first, second = pair_cols[...], other_cols[...]
    even = lax.axis_index("col") % 2 == 0
    low_cols, high_cols = jnp.where(even, second, first), jnp.where(even, first, second)
    at = iota(strip_low.shape, 0)
    low, high = strip_low[...], strip_high[...]
    low = jnp.where(at == 2 * nr, low_cols[0:1], jnp.where(at == 2 * nr + 1, high_cols[0:1], low))
    high = jnp.where(at == 2 * nr + 1, high_cols[rows - 1 : rows], high)
    even = lax.axis_index("tile") % 2 == 0
    for_pairs[...] = jnp.where(even, high, low)
    for_others[...] = jnp.where(even, low, high)


def inner_kernel(weighted, gain, pair_cols, other_cols, image, q_low, q_high, g_low, g_high, k_low, k_high, pack, sums, again):
    count, rows, width = weighted.shape
    even = lax.axis_index("col") % 2 == 0
    first, second = pair_cols[0:rows], other_cols[0:rows]
    pack_low, pack_high = jnp.where(even, second, first), jnp.where(even, first, second)
    lane = iota((rows, LANES), 1)
    zero = [jnp.zeros((rows, LANES), jnp.float32) for _ in range(width // LANES)]
    one = jnp.zeros((8, LANES), jnp.float32)

    def applied(read, columns, emit, carry):
        def step(k, state):
            side_before, level_twice, level_before, carry = state
            tiles = tiles_of(read[k])
            side = sides(tiles, *columns(k))
            level = levels(tiles, side)
            found = [s + a + b for s, a, b in zip(side_before, level_twice, level)]
            return side, level_before, level, emit(k - 1, found, carry)

        tiles = tiles_of(read[0])
        side = sides(tiles, *columns(0))
        state = (side, zero, levels(tiles, side), carry)
        side, level_twice, _, carry = lax.fori_loop(1, count, step, state, unroll=3)
        return emit(count - 1, [s + a for s, a in zip(side, level_twice)], carry)

    def outside(k):
        return pltpu.roll(pack_low, lax.rem(LANES - k, LANES), 1), pltpu.roll(pack_high, LANES - 1 - k, 1)

    def first_image(k, found, carry):
        packed, zb, bb = carry
        u, g = tiles_of(weighted[k]), tiles_of(gain[k])
        ub = [a * b for a, b in zip(g, found)]
        for i, (q, v) in enumerate(zip(found, ub)):
            image[k, :, i * LANES : (i + 1) * LANES] = q
            again[k, :, i * LANES : (i + 1) * LANES] = v
        keep_rows(k, found, q_low, q_high, count)
        keep_rows(k, g, g_low, g_high, count)
        packed = jnp.where(lane == k, pltpu.roll(ub[-1], k + 1, 1), packed)
        return packed, zb + dot(u, found), bb + dot(ub, found)

    packed, zb, bb = applied(weighted, outside, first_image, (zero[0], one, one))
    pack[...] = packed

    def second_image(k, found, bbb):
        keep_rows(k, found, k_low, k_high, count)
        return bbb + dot(tiles_of(again[k]), found)

    bbb = applied(again, lambda k: (None, None), second_image, one)
    sums[0], sums[1], sums[2] = zb, bb, bbb


def shifts(values, axis):
    size = values.shape[axis]
    place = iota(values.shape, axis)
    up = jnp.where(place == size - 1, 0.0, turned(values, -1, axis))
    down = jnp.where(place == 0, 0.0, turned(values, 1, axis))
    return up + down


def near(values, axis):
    return values + weight_cross * shifts(values, axis)


def along(tiles, left, right):
    lane = iota(tiles[0].shape, 1)
    ahead = [turned(tile, -1, 1) for tile in tiles] + [right]
    behind = [left] + [turned(tile, 1, 1) for tile in tiles]
    return [
        jnp.where(lane == LANES - 1, ahead[i + 1], ahead[i]) + jnp.where(lane == 0, behind[i], behind[i + 1])
        for i in range(len(tiles))
    ]


def finish_kernel(
    pair_strip,
    other_strip,
    strip_low,
    strip_high,
    q_low,
    q_high,
    g_low,
    g_high,
    k_low,
    k_high,
    pack,
    cols_high,
    pair_cols,
    other_cols,
    prof,
    sum_zz,
    sum_rest,
    out,
    add_low,
    add_high,
):
    count = prof.shape[0]
    nr = q_low.shape[0]
    tiles = nr // count
    rows = pack.shape[0]
    even = lax.axis_index("tile") % 2 == 0
    first, second = pair_strip[...], other_strip[...]
    low, high = jnp.where(even, second, first), jnp.where(even, first, second)
    even = lax.axis_index("col") % 2 == 0
    high_cols = jnp.where(even, pair_cols[...], other_cols[...])

    def blocks(values, start=0):
        return [values[start + i * count : start + (i + 1) * count] for i in range(tiles)]

    shape = (count, LANES)
    diagonal = iota(shape, 0) == iota(shape, 1)

    def to_column(line):
        return jnp.sum(jnp.where(diagonal, line, 0.0), axis=1, keepdims=True)

    def to_line(column):
        return jnp.sum(jnp.where(diagonal, column, 0.0), axis=0, keepdims=True)

    def total(left, right):
        return dot(left, right)

    zb, bb, bbb = sum_rest[0], sum_rest[1], sum_rest[2]
    outer = []
    for halo, u, q, g, ka, add in (
        (low, strip_low, q_low, g_low, k_low, add_low),
        (high, strip_high, q_high, g_high, k_high, add_high),
    ):
        h = [near(block, 0) for block in blocks(halo)]
        for i, block in enumerate(h):
            add[i * count : (i + 1) * count, :] = block
        u, q, g, ka = blocks(u[...]), blocks(q[...]), blocks(g[...]), blocks(ka[...])
        e = [a * b for a, b in zip(g, h)]
        side = along(e, 0.0, 0.0)
        ke = [s + shifts(weight_vert * a + weight_cross * s, 0) for a, s in zip(e, side)]
        zb = zb + total(u, h)
        bb = bb + total(e, [2.0 * a + b for a, b in zip(q, h)])
        bbb = bbb + total(e, [2.0 * a + b for a, b in zip(ka, ke)])
        outer.append((u, e, [a * b + c for a, b, c in zip(g, q, e)]))
    (_, e_low, _), (u_last, e_high, ub_last) = outer

    u_next, u_after = blocks(high), blocks(high, nr)
    side = along(u_next, to_column(high[2 * nr : 2 * nr + 1]), to_column(high[2 * nr + 1 : 2 * nr + 2]))
    side = [s + a + b for s, a, b in zip(side, u_last, u_after)]
    q_next = [s + shifts(weight_vert * a + weight_cross * s, 0) for a, s in zip(u_next, side)]
    level = prof[...]
    for i in range(tiles):
        g, _ = gains(level * high[2 * nr + 2 + i : 2 * nr + 3 + i])
        bbb = bbb + 2.0 * folded(ub_last[i] * near(g * q_next[i], 0))

    lane, row = iota((rows, LANES), 1), iota((rows, LANES), 0)
    held = lane < count
    u_next = jnp.where(held, high_cols[0:rows], 0.0)
    up = jnp.where(row == 0, jnp.where(held, low[2 * nr + 1 : 2 * nr + 2], 0.0), turned(u_next, 1, 0))
    down = jnp.where(row == rows - 1, jnp.where(held, high[2 * nr + 1 : 2 * nr + 2], 0.0), turned(u_next, -1, 0))
    side = cols_high[0:rows] + high_cols[rows:] + up + down
    q_next = side + shifts(weight_vert * u_next + weight_cross * side, 1)
    g, _ = gains(to_line(level) * high_cols[0:rows, LANES - 1 :])
    ub = pack[...]
    ub = ub + jnp.where(row == 0, to_line(e_low[-1][:, LANES - 1 :]), 0.0)
    ub = ub + jnp.where(row == rows - 1, to_line(e_high[-1][:, LANES - 1 :]), 0.0)
    bbb = bbb + 2.0 * folded(ub * near(g * q_next, 1))

    layer = lax.axis_index("layer")
    out[...] = jnp.zeros_like(out)
    for i, values in enumerate((sum_zz[...], zb, bb, bbb)):
        out[pl.ds(8 * layer + i, 1), :] = jnp.sum(values, axis=0, keepdims=True)


def ready_kernel(source, profile_own, profile_other, column, error, image, add_low, add_high, base, kept, sent):
    layer = lax.axis_index("layer")
    half, rows, width = source.shape[1:]
    count = 2 * half
    mine = column[...] * multiplier_of(error, layer)
    theirs = column[...] * multiplier_of(error, 1 - layer)
    row = iota((rows, LANES), 0)

    def store(ref, where, scale, k):
        scale, plane = tiles_of(scale), tiles_of(image[k])
        for i, q in enumerate(plane):
            q = q + jnp.where(row == 0, add_low[pl.ds(i * count + k, 1), :], 0.0)
            q = q + jnp.where(row == rows - 1, add_high[pl.ds(i * count + k, 1), :], 0.0)
            ref[where, :, i * LANES : (i + 1) * LANES] = scale[i] * q

    def step(at, _):
        _, scale = gains(profile_other[at] * mine)
        store(sent, at, scale, (1 - layer) * half + at)
        _, scale = gains(profile_own[at] * mine)
        store(kept, at, scale, layer * half + at)
        base[layer, at] = scale * (source_scale * source[layer, at])
        _, scale = gains(profile_own[at] * theirs)
        base[1 - layer, at] = scale * (source_scale * source[1 - layer, at])
        return 0

    lax.fori_loop(0, half, step, 0, unroll=2)


def final_kernel(base, kept, received, sums, out, factors):
    layer = lax.axis_index("layer")
    which, at = pl.program_id(0), pl.program_id(1)
    size, rows, width = out.shape[1:]

    @pl.when((which == 0) & (at == 0))
    def _():
        for each in range(2):
            values = jnp.sum(sums[8 * each : 8 * each + 8], axis=1, keepdims=True)
            zz, zb, bb, bbb = (values[i : i + 1] for i in range(4))
            delta = zz - zb
            alpha = zz / delta
            rest = -zb / delta
            beta = (zz * bb - zb * zb) / (delta * delta)
            gamma = zz * beta
            delta_next = gamma - (rest * rest * zb + 2.0 * alpha * rest * bb + alpha * alpha * bbb)
            alpha_next = gamma / (delta_next - beta * gamma / alpha)
            factors[each, 0] = jnp.broadcast_to(alpha + alpha_next * (rest + beta), (8, LANES))
            factors[each, 1] = jnp.broadcast_to(alpha_next * alpha, (8, LANES))

    first = jnp.broadcast_to(factors[which, 0][0:1, 0:1], (rows, width))
    second = jnp.broadcast_to(factors[which, 1][0:1, 0:1], (rows, width))

    def fill(image):
        for i in range(size):
            k = at * size + i
            out[0, i] = first * base[which, k] + second * image[k]

    @pl.when(which == layer)
    def _():
        fill(kept)

    @pl.when(which != layer)
    def _():
        fill(received)


VMEM = pl.BlockSpec(memory_space=pltpu.VMEM)
SMEM = pl.BlockSpec(memory_space=pltpu.SMEM)


def call(kernel, out_shape, args, name, scalars=(), scratch=(), aliases=None, cost=0):
    return pl.pallas_call(
        kernel,
        out_shape=[jax.ShapeDtypeStruct(shape, jnp.float32) for shape in out_shape],
        in_specs=[SMEM if i in scalars else VMEM for i in range(len(args))],
        out_specs=[VMEM] * len(out_shape),
        scratch_shapes=[pltpu.VMEM(shape, jnp.float32) for shape in scratch],
        input_output_aliases=aliases or {},
        compiler_params=pltpu.CompilerParams(vmem_limit_bytes=GRANT),
        cost_estimate=pl.CostEstimate(flops=cost, bytes_accessed=cost, transcendentals=0) if cost else None,
        name=name,
    )(*args)


def local(source, profile, column, terrain_height_error):
    copies, half, rows, width = source.shape
    count, tiles = 2 * half, width // LANES
    assert lax.axis_size("layer") == copies == 2 and count < LANES and width % LANES == 0
    assert count % 8 == 0 and rows % 8 == 0 and rows > 2
    swap = [(0, 1), (1, 0)]
    other = lax.ppermute(source, "layer", swap)
    profile_other = lax.ppermute(profile, "layer", swap)
    nr = tiles * count
    block, row, pack = (count, rows, width), (nr, LANES), (rows, LANES)
    strip = (-(-(2 * nr + 2 + tiles) // 8) * 8, LANES)
    shapes = [block, block, strip, strip, (2 * rows, LANES), (2 * rows, LANES), (count, LANES), (8, LANES)]
    begun = call(
        functools.partial(weighted_kernel, True),
        shapes,
        (source, profile, column, terrain_height_error),
        "weighted_own",
        (1,),
    )
    weighted, gain, strip_low, strip_high, cols_low, cols_high, prof, sum_zz = call(
        functools.partial(weighted_kernel, False),
        shapes,
        (other, profile_other, column, terrain_height_error, *begun),
        "weighted_other",
        (1,),
        aliases={4 + i: i for i in range(8)},
    )
    even = lax.axis_index("col") % 2 == 0
    pair_cols, other_cols = exchanged(
        jnp.where(even, cols_high, cols_low), jnp.where(even, cols_low, cols_high), "col"
    )
    for_pairs, for_others = call(
        functools.partial(join_kernel, nr), [strip, strip], (strip_low, strip_high, pair_cols, other_cols), "join"
    )
    pair_strip, other_strip = exchanged(for_pairs, for_others, "tile")
    image, q_low, q_high, g_low, g_high, k_low, k_high, packed, sum_rest = call(
        inner_kernel,
        [block, row, row, row, row, row, row, pack, (3, 8, LANES)],
        (weighted, gain, pair_cols, other_cols),
        "inner",
        scratch=(block,),
    )
    sums, add_low, add_high = call(
        finish_kernel,
        [(16, LANES), row, row],
        (
            pair_strip,
            other_strip,
            strip_low,
            strip_high,
            q_low,
            q_high,
            g_low,
            g_high,
            k_low,
            k_high,
            packed,
            cols_high,
            pair_cols,
            other_cols,
            prof,
            sum_zz,
            sum_rest,
        ),
        "finish",
    )
    part = (half, rows, width)
    base, kept, sent = call(
        ready_kernel,
        [source.shape, part, part],
        (source, profile, profile_other, column, terrain_height_error, image, add_low, add_high),
        "ready",
        (1, 2),
    )
    received = lax.ppermute(sent, "layer", swap)
    sums = total(sums)
    size = half // 2 if half % 2 == 0 else half
    return pl.pallas_call(
        final_kernel,
        out_shape=jax.ShapeDtypeStruct(source.shape, jnp.float32),
        grid=(2, half // size),
        in_specs=[VMEM] * 4,
        out_specs=pl.BlockSpec((1, size, rows, width), lambda i, j: (i, j, 0, 0)),
        scratch_shapes=[pltpu.VMEM((2, 2, 8, LANES), jnp.float32)],
        compiler_params=pltpu.CompilerParams(vmem_limit_bytes=GRANT),
        name="final",
    )(base, kept, received, sums)


def solution(mesh):
    placed = (
        P("group", "layer", "tile", "col"),
        P("layer"),
        P(("group", "tile"), "col"),
        P("group", "tile", "col"),
    )
    return jax.shard_map(
        local,
        mesh=mesh,
        in_specs=placed,
        out_specs=P("group", "layer", "tile", "col"),
        check_vma=False,
    )
```

```python
import functools

import jax
import jax.numpy as jnp
from jax import lax
from jax.experimental import pallas as pl
from jax.experimental.pallas import tpu as pltpu
from jax.sharding import PartitionSpec as P


weight_vert = 2.0
weight_cross = 0.3
gain_bound = 1.6
total_weight = 10.4
diag_shift = 0.5
source_scale = 8.0

LANES = 128
GRANT = 8 << 20


def line_pairs(count, first):
    pairs = []
    for low in range(first, count - 1, 2):
        pairs += [(low, low + 1), (low + 1, low)]
    return pairs


def exchanged(for_pairs, for_others, axis):
    count = lax.axis_size(axis)
    if count == 1:
        return jnp.zeros_like(for_pairs), jnp.zeros_like(for_others)
    first = lax.ppermute(for_pairs, axis, line_pairs(count, 0))
    if count == 2:
        return first, jnp.zeros_like(first)
    return first, lax.ppermute(for_others, axis, line_pairs(count, 1))


def flipped(values, sizes, axes, bits):
    shape = [sizes[axis] for axis in axes]
    pairs = []
    for flat in range(functools.reduce(lambda a, b: a * b, shape, 1)):
        place, rest = [], flat
        for size in reversed(shape):
            place.insert(0, rest % size)
            rest //= size
        target = 0
        for where, size, bit in zip(place, shape, bits):
            target = target * size + (where ^ bit)
        pairs.append((flat, target))
    return lax.ppermute(values, axes, pairs)


def total(values):
    sizes = {axis: lax.axis_size(axis) for axis in ("layer", "col", "tile")}
    assert all(size & (size - 1) == 0 for size in sizes.values())
    first = 1
    if sizes["col"] > 1 and sizes["layer"] == 2:
        values = (
            values
            + flipped(values, sizes, ("layer",), (1,))
            + flipped(values, sizes, ("col",), (1,))
            + flipped(values, sizes, ("col", "layer"), (1, 1))
        )
        first = 2
    else:
        values = values + flipped(values, sizes, ("layer",), (1,))

    def later(values):
        for axis, bit in (("col", first), ("tile", 1)):
            while bit < sizes[axis]:
                values = values + flipped(values, sizes, (axis,), (bit,))
                bit *= 2
        return values

    return values, later


def tiles_of(plane):
    return [plane[:, at : at + LANES] for at in range(0, plane.shape[1], LANES)]


def iota(shape, axis):
    return lax.broadcasted_iota(jnp.int32, shape, axis)


def turned(values, by, axis):
    by %= values.shape[axis]
    return pltpu.roll(values, by, axis) if by else values


def sides(tiles):
    rows, lanes = tiles[0].shape
    row, lane = iota((rows, lanes), 0), iota((rows, lanes), 1)
    ahead = [turned(tile, -1, 1) for tile in tiles] + [0.0]
    behind = [0.0] + [turned(tile, 1, 1) for tile in tiles]
    out = []
    for i, tile in enumerate(tiles):
        below = jnp.where(row == rows - 1, 0.0, turned(tile, -1, 0))
        above = jnp.where(row == 0, 0.0, turned(tile, 1, 0))
        right = jnp.where(lane == lanes - 1, ahead[i + 1], ahead[i])
        left = jnp.where(lane == 0, behind[i], behind[i + 1])
        out.append((below + above) + (right + left))
    return out


def levels(tiles, side):
    return [weight_vert * tile + weight_cross * s for tile, s in zip(tiles, side)]


def gains(metric):
    scale = metric / (gain_bound * total_weight * metric + diag_shift)
    return metric * scale, scale


def folded(values):
    return functools.reduce(lambda a, b: a + b, [values[at : at + 8] for at in range(0, values.shape[0], 8)])


def dot(left, right):
    return functools.reduce(lambda a, b: a + b, [folded(a * b) for a, b in zip(left, right)])


def keep_rows(k, tiles, low, high, count):
    rows = tiles[0].shape[0]
    for i, tile in enumerate(tiles):
        if low is not None:
            low[pl.ds(i * count + k, 1), :] = tile[0:1]
        if high is not None:
            high[pl.ds(i * count + k, 1), :] = tile[rows - 1 : rows]


def weigh(base, read, profile, columns, carry, refs):
    weighted, gain, strip_low, strip_high, prof = refs
    rows, width = columns.shape
    count, tiles = weighted.shape[0], width // LANES
    lane = iota((rows, LANES), 1)

    def step(at, carry):
        first, second, last, acc = carry
        k = base + at
        g, _ = gains(profile[at] * columns)
        forcing = source_scale * read(at)
        u = g * forcing
        weighted[k] = u
        gain[k] = g
        parts = tiles_of(u)
        keep_rows(k, parts, strip_low, strip_high, count)
        for i, part in enumerate(parts):
            strip_low[pl.ds((tiles + i) * count + k, 1), :] = part[1:2]
        prof[pl.ds(k, 1), :] = jnp.full((1, LANES), profile[at])
        first = jnp.where(lane == k, pltpu.roll(parts[0], k, 1), first)
        second = jnp.where(lane == k, pltpu.roll(parts[0], lax.rem(k + LANES - 1, LANES), 1), second)
        last = jnp.where(lane == k, pltpu.roll(parts[-1], k + 1, 1), last)
        return first, second, last, acc + dot(parts, tiles_of(forcing))

    return lax.fori_loop(0, weighted.shape[0] // 2, step, carry, unroll=5)


def own_kernel(
    source, profile, factors, weighted, gain, strip_low, strip_high, cols_low, cols_high, prof, sums
):
    layer = lax.axis_index("layer")
    half, rows, width = source.shape[1:]
    count, tiles = 2 * half, width // LANES
    columns = factors[layer]
    lane = iota((rows, LANES), 1)
    zeros = jnp.zeros((rows, LANES), jnp.float32)
    edge = tiles_of(columns)
    carry = (jnp.where(lane == LANES - 1, turned(edge[0], -1, 1), 0.0), zeros, zeros, jnp.zeros((8, LANES), jnp.float32))
    for i, tile in enumerate(edge):
        strip_low[2 * tiles * count + 2 + i : 2 * tiles * count + 3 + i, :] = tile[0:1]
    first, second, last, acc = weigh(
        layer * half,
        lambda at: source[layer, at],
        profile,
        columns,
        carry,
        (weighted, gain, strip_low, strip_high, prof),
    )
    cols_low[0:rows] = first
    cols_low[rows:] = second
    cols_high[0:rows] = last
    cols_high[rows:] = jnp.zeros_like(last)
    sums[...] = acc


def other_kernel(source, profile, factors, *refs):
    low, high, acc = refs[4], refs[5], refs[7]
    weighted, gain, strip_low, strip_high, cols_low, cols_high, prof, sums = refs[8:]
    layer = lax.axis_index("layer")
    half, rows = source.shape[1:3]
    carry = (low[0:rows], low[rows:], high[0:rows], acc[...])
    first, second, last, acc = weigh(
        (1 - layer) * half,
        lambda at: source[layer, at],
        profile,
        factors[layer],
        carry,
        (weighted, gain, strip_low, strip_high, prof),
    )
    cols_low[0:rows] = first
    cols_low[rows:] = second
    cols_high[0:rows] = last
    cols_high[rows:] = jnp.zeros_like(last)
    sums[...] = acc


def join_kernel(nr, strip_low, strip_high, pair_cols, other_cols, for_pairs, for_others):
    rows = pair_cols.shape[0] // 2
    first, second = pair_cols[...], other_cols[...]
    even = lax.axis_index("col") % 2 == 0
    low_cols, high_cols = jnp.where(even, second, first), jnp.where(even, first, second)
    at = iota(strip_low.shape, 0)
    low, high = strip_low[...], strip_high[...]
    low = jnp.where(at == 2 * nr, low_cols[0:1], jnp.where(at == 2 * nr + 1, high_cols[0:1], low))
    high = jnp.where(at == 2 * nr + 1, high_cols[rows - 1 : rows], high)
    even = lax.axis_index("tile") % 2 == 0
    for_pairs[...] = jnp.where(even, high, low)
    for_others[...] = jnp.where(even, low, high)


def shifts(values, axis):
    size = values.shape[axis]
    place = iota(values.shape, axis)
    up = jnp.where(place == size - 1, 0.0, turned(values, -1, axis))
    down = jnp.where(place == 0, 0.0, turned(values, 1, axis))
    return up + down


def near(values, axis):
    return values + weight_cross * shifts(values, axis)


def swept(count, width, rows, plane, emit, carry):
    zero = [jnp.zeros((rows, LANES), jnp.float32) for _ in range(width // LANES)]

    def step(k, state):
        side_before, level_twice, level_before, carry = state
        tiles, carry = plane(k, carry)
        side = sides(tiles)
        level = levels(tiles, side)
        found = [s + a + b for s, a, b in zip(side_before, level_twice, level)]
        return side, level_before, level, emit(k - 1, found, carry)

    tiles, carry = plane(0, carry)
    side = sides(tiles)
    state = (side, zero, levels(tiles, side), carry)
    side, level_twice, _, carry = lax.fori_loop(1, count, step, state, unroll=13)
    return emit(count - 1, [s + a for s, a in zip(side, level_twice)], carry)


def put(ref, k, tiles):
    for i, tile in enumerate(tiles):
        ref[k, :, i * LANES : (i + 1) * LANES] = tile


def image_kernel(weighted, gain, image, g_low, g_high):
    count, rows, width = weighted.shape

    def plane(k, carry):
        return tiles_of(weighted[k]), carry

    def emit(k, found, carry):
        put(image, k, found)
        keep_rows(k, tiles_of(gain[k]), g_low, g_high, count)
        return carry

    swept(count, width, rows, plane, emit, 0)


def inner_kernel(begun, weighted, gain, pair_cols, other_cols, image, q_low, q_high, k_low, k_high, pack, sums, again):
    count, rows, width = weighted.shape
    even = lax.axis_index("col") % 2 == 0
    lane = iota((rows, LANES), 1)
    first, second = pair_cols[0:rows], other_cols[0:rows]
    add_low = near(jnp.where((lane < count), jnp.where(even, second, first), 0.0), 1)
    add_high = near(jnp.where((lane < count), jnp.where(even, first, second), 0.0), 1)
    one = jnp.zeros((8, LANES), jnp.float32)

    def plane(k, carry):
        packed, zb, bb, bbb = carry
        u, g, q = tiles_of(weighted[k]), tiles_of(gain[k]), tiles_of(begun[k])
        q[0] = q[0] + jnp.where(lane == 0, pltpu.roll(add_low, lax.rem(LANES - k, LANES), 1), 0.0)
        q[-1] = q[-1] + jnp.where(lane == LANES - 1, pltpu.roll(add_high, LANES - 1 - k, 1), 0.0)
        ub = [a * b for a, b in zip(g, q)]
        put(image, k, q)
        put(again, k, ub)
        keep_rows(k, q, q_low, q_high, count)
        packed = jnp.where(lane == k, pltpu.roll(ub[-1], (k + 1) % LANES, 1), packed)
        return ub, (packed, zb + dot(u, q), bb + dot(ub, q), bbb)

    def emit(k, found, carry):
        keep_rows(k, found, k_low, k_high, count)
        return *carry[:3], carry[3] + dot(tiles_of(again[k]), found)

    packed, zb, bb, bbb = swept(count, width, rows, plane, emit, (jnp.zeros((rows, LANES), jnp.float32), one, one, one))
    pack[...] = packed
    sums[0], sums[1], sums[2] = zb, bb, bbb


def along(tiles, left, right):
    lane = iota(tiles[0].shape, 1)
    ahead = [turned(tile, -1, 1) for tile in tiles] + [right]
    behind = [left] + [turned(tile, 1, 1) for tile in tiles]
    return [
        jnp.where(lane == LANES - 1, ahead[i + 1], ahead[i]) + jnp.where(lane == 0, behind[i], behind[i + 1])
        for i in range(len(tiles))
    ]


def finish_kernel(
    pair_strip,
    other_strip,
    strip_low,
    strip_high,
    q_low,
    q_high,
    g_low,
    g_high,
    k_low,
    k_high,
    pack,
    cols_high,
    pair_cols,
    other_cols,
    prof,
    sum_zz,
    sum_rest,
    out,
    add_low,
    add_high,
):
    count = prof.shape[0]
    nr = q_low.shape[0]
    tiles = nr // count
    rows = pack.shape[0]
    even = lax.axis_index("tile") % 2 == 0
    first, second = pair_strip[...], other_strip[...]
    low, high = jnp.where(even, second, first), jnp.where(even, first, second)
    even = lax.axis_index("col") % 2 == 0
    high_cols = jnp.where(even, pair_cols[...], other_cols[...])

    def blocks(values, start=0):
        return [values[start + i * count : start + (i + 1) * count] for i in range(tiles)]

    shape = (count, LANES)
    diagonal = iota(shape, 0) == iota(shape, 1)

    def to_column(line):
        return jnp.sum(jnp.where(diagonal, line, 0.0), axis=1, keepdims=True)

    def to_line(column):
        return jnp.sum(jnp.where(diagonal, column, 0.0), axis=0, keepdims=True)

    def total(left, right):
        return dot(left, right)

    zb, bb, bbb = sum_rest[0], sum_rest[1], sum_rest[2]
    outer = []
    for halo, u, q, g, ka, add in (
        (low, strip_low, q_low, g_low, k_low, add_low),
        (high, strip_high, q_high, g_high, k_high, add_high),
    ):
        h = [near(block, 0) for block in blocks(halo)]
        for i, block in enumerate(h):
            add[i * count : (i + 1) * count, :] = block
        u, q, g, ka = blocks(u[...]), blocks(q[...]), blocks(g[...]), blocks(ka[...])
        e = [a * b for a, b in zip(g, h)]
        side = along(e, 0.0, 0.0)
        ke = [s + shifts(weight_vert * a + weight_cross * s, 0) for a, s in zip(e, side)]
        zb = zb + total(u, h)
        bb = bb + total(e, [2.0 * a + b for a, b in zip(q, h)])
        bbb = bbb + total(e, [2.0 * a + b for a, b in zip(ka, ke)])
        outer.append((u, e, [a * b + c for a, b, c in zip(g, q, e)]))
    (_, e_low, _), (u_last, e_high, ub_last) = outer

    u_next, u_after = blocks(high), blocks(high, nr)
    side = along(u_next, to_column(high[2 * nr : 2 * nr + 1]), to_column(high[2 * nr + 1 : 2 * nr + 2]))
    side = [s + a + b for s, a, b in zip(side, u_last, u_after)]
    q_next = [s + shifts(weight_vert * a + weight_cross * s, 0) for a, s in zip(u_next, side)]
    level = prof[...]
    for i in range(tiles):
        g, _ = gains(level * high[2 * nr + 2 + i : 2 * nr + 3 + i])
        bbb = bbb + 2.0 * folded(ub_last[i] * near(g * q_next[i], 0))

    lane, row = iota((rows, LANES), 1), iota((rows, LANES), 0)
    held = lane < count
    u_next = jnp.where(held, high_cols[0:rows], 0.0)
    up = jnp.where(row == 0, jnp.where(held, low[2 * nr + 1 : 2 * nr + 2], 0.0), turned(u_next, 1, 0))
    down = jnp.where(row == rows - 1, jnp.where(held, high[2 * nr + 1 : 2 * nr + 2], 0.0), turned(u_next, -1, 0))
    side = cols_high[0:rows] + high_cols[rows:] + up + down
    q_next = side + shifts(weight_vert * u_next + weight_cross * side, 1)
    g, _ = gains(to_line(level) * high_cols[0:rows, LANES - 1 :])
    ub = pack[...]
    ub = ub + jnp.where(row == 0, to_line(e_low[-1][:, LANES - 1 :]), 0.0)
    ub = ub + jnp.where(row == rows - 1, to_line(e_high[-1][:, LANES - 1 :]), 0.0)
    bbb = bbb + 2.0 * folded(ub * near(g * q_next, 1))

    layer = lax.axis_index("layer")
    out[...] = jnp.zeros_like(out)
    for i, values in enumerate((sum_zz[...], zb, bb, bbb)):
        out[pl.ds(8 * layer + i, 1), :] = jnp.sum(values, axis=0, keepdims=True)


def ready_kernel(source, profile_own, profile_other, factors, image, add_low, add_high, _, base, kept, sent):
    layer = lax.axis_index("layer")
    half, rows, _ = source.shape[1:]
    count = 2 * half
    mine, theirs = factors[layer], factors[1 - layer]
    row = iota((rows, LANES), 0)

    def store(ref, where, scale, k):
        scale, plane = tiles_of(scale), tiles_of(image[k])
        for i, q in enumerate(plane):
            q = q + jnp.where(row == 0, add_low[pl.ds(i * count + k, 1), :], 0.0)
            q = q + jnp.where(row == rows - 1, add_high[pl.ds(i * count + k, 1), :], 0.0)
            ref[where, :, i * LANES : (i + 1) * LANES] = scale[i] * q

    def step(at, _):
        _, scale = gains(profile_other[at] * mine)
        store(sent, at, scale, (1 - layer) * half + at)
        _, scale = gains(profile_own[at] * mine)
        store(kept, at, scale, layer * half + at)
        base[layer, at] = scale * (source_scale * source[layer, at])
        _, scale = gains(profile_own[at] * theirs)
        base[1 - layer, at] = scale * (source_scale * source[1 - layer, at])
        return 0

    lax.fori_loop(0, half, step, 0, unroll=4)


def final_kernel(base, kept, received, sums, out, factors):
    layer = lax.axis_index("layer")
    which, at = pl.program_id(0), pl.program_id(1)
    size, rows, width = out.shape[1:]

    @pl.when((which == 0) & (at == 0))
    def _():
        for each in range(2):
            values = jnp.sum(sums[8 * each : 8 * each + 8], axis=1, keepdims=True)
            zz, zb, bb, bbb = (values[i : i + 1] for i in range(4))
            delta = zz - zb
            alpha = zz / delta
            rest = -zb / delta
            beta = (zz * bb - zb * zb) / (delta * delta)
            gamma = zz * beta
            delta_next = gamma - (rest * rest * zb + 2.0 * alpha * rest * bb + alpha * alpha * bbb)
            alpha_next = gamma / (delta_next - beta * gamma / alpha)
            factors[each, 0] = jnp.broadcast_to(alpha + alpha_next * (rest + beta), (8, LANES))
            factors[each, 1] = jnp.broadcast_to(alpha_next * alpha, (8, LANES))

    first = jnp.broadcast_to(factors[which, 0][0:1, 0:1], (rows, width))
    second = jnp.broadcast_to(factors[which, 1][0:1, 0:1], (rows, width))

    def fill(image):
        for i in range(size):
            k = at * size + i
            out[0, i] = first * base[which, k] + second * image[k]

    @pl.when(which == layer)
    def _():
        fill(kept)

    @pl.when(which != layer)
    def _():
        fill(received)


VMEM = pl.BlockSpec(memory_space=pltpu.VMEM)
SMEM = pl.BlockSpec(memory_space=pltpu.SMEM)


def call(kernel, out_shape, args, scalars=(), scratch=(), aliases=None, cost=0):
    return pl.pallas_call(
        kernel,
        out_shape=[jax.ShapeDtypeStruct(shape, jnp.float32) for shape in out_shape],
        in_specs=[SMEM if i in scalars else VMEM for i in range(len(args))],
        out_specs=[VMEM] * len(out_shape),
        scratch_shapes=[pltpu.VMEM(shape, jnp.float32) for shape in scratch],
        input_output_aliases=aliases or {},
        compiler_params=pltpu.CompilerParams(vmem_limit_bytes=GRANT),
        cost_estimate=pl.CostEstimate(flops=cost, bytes_accessed=cost, transcendentals=0) if cost else None,
    )(*args)


def solve(source, profile, column, terrain_height_error):
    copies, half, rows, width = source.shape
    count, tiles = 2 * half, width // LANES
    assert lax.axis_size("layer") == copies == 2 and count < LANES and width % LANES == 0
    assert count % 8 == 0 and rows % 8 == 0 and rows > 2
    swap = [(0, 1), (1, 0)]
    other = lax.ppermute(source, "layer", swap)
    profile_other = lax.ppermute(profile, "layer", swap)
    nr = tiles * count
    block, row, pack = (count, rows, width), (nr, LANES), (rows, LANES)
    strip = (-(-(2 * nr + 2 + tiles) // 8) * 8, LANES)
    shapes = [block, block, strip, strip, (2 * rows, LANES), (2 * rows, LANES), (count, LANES), (8, LANES)]
    factors = column * (1.0 + 0.002 * terrain_height_error.astype(jnp.float32))
    begun = call(own_kernel, shapes, (source, profile, factors), (1,))
    weighted, gain, strip_low, strip_high, cols_low, cols_high, prof, sum_zz = call(
        other_kernel, shapes, (other, profile_other, factors, *begun), (1,), aliases={3 + i: i for i in range(8)}
    )
    even = lax.axis_index("col") % 2 == 0
    pair_cols, other_cols = exchanged(
        jnp.where(even, cols_high, cols_low), jnp.where(even, cols_low, cols_high), "col"
    )
    image, g_low, g_high = call(image_kernel, [block, row, row], (weighted, gain))
    for_pairs, for_others = call(
        functools.partial(join_kernel, nr), [strip, strip], (strip_low, strip_high, pair_cols, other_cols)
    )
    pair_strip, other_strip = exchanged(for_pairs, for_others, "tile")
    image, q_low, q_high, k_low, k_high, packed, sum_rest = call(
        inner_kernel,
        [block, row, row, row, row, pack, (3, 8, LANES)],
        (image, weighted, gain, pair_cols, other_cols),
        scratch=(block,),
    )
    sums, add_low, add_high = call(
        finish_kernel,
        [(16, LANES), row, row],
        (
            pair_strip,
            other_strip,
            strip_low,
            strip_high,
            q_low,
            q_high,
            g_low,
            g_high,
            k_low,
            k_high,
            packed,
            cols_high,
            pair_cols,
            other_cols,
            prof,
            sum_zz,
            sum_rest,
        ),
    )
    part = (half, rows, width)
    sums, later = total(sums)
    base, kept, sent = call(
        ready_kernel,
        [source.shape, part, part],
        (source, profile, profile_other, factors, image, add_low, add_high, sums),
        (1, 2),
    )
    received = lax.ppermute(sent, "layer", swap)
    sums = later(sums)
    size = half // 2 if half % 2 == 0 else half
    return pl.pallas_call(
        final_kernel,
        out_shape=jax.ShapeDtypeStruct(source.shape, jnp.float32),
        grid=(2, half // size),
        in_specs=[VMEM] * 4,
        out_specs=pl.BlockSpec((1, size, rows, width), lambda i, j: (i, j, 0, 0)),
        scratch_shapes=[pltpu.VMEM((2, 2, 8, LANES), jnp.float32)],
        compiler_params=pltpu.CompilerParams(vmem_limit_bytes=GRANT),
        name="final",
    )(base, kept, received, sums)


def solution(mesh):
    placed = (
        P("group", "layer", "tile", "col"),
        P("layer"),
        P(("group", "tile"), "col"),
        P("group", "tile", "col"),
    )
    return jax.shard_map(
        solve,
        mesh=mesh,
        in_specs=placed,
        out_specs=P("group", "layer", "tile", "col"),
        check_vma=False,
    )
```

```python
import functools

import jax
import jax.numpy as jnp
from jax import lax
from jax.experimental import pallas as pl
from jax.experimental.pallas import tpu as pltpu
from jax.sharding import PartitionSpec as P


weight_vert = 2.0
weight_cross = 0.3
gain_bound = 1.6
total_weight = 10.4
diag_shift = 0.5
source_scale = 8.0

LANES = 128
GRANT = 8 << 20


def line_pairs(count, first):
    pairs = []
    for low in range(first, count - 1, 2):
        pairs += [(low, low + 1), (low + 1, low)]
    return pairs


def exchanged(for_pairs, for_others, axis):
    count, layers = lax.axis_size(axis), lax.axis_size("layer")
    received = []
    for first, values in ((0, for_pairs), (1, for_others)):
        partner = dict(line_pairs(count, first))
        if not partner:
            received.append(jnp.zeros_like(values))
            continue
        pairs = []
        for place in range(count):
            for layer in range(layers):
                target = (partner[place], layer) if place in partner else (place, layers - 1 - layer)
                pairs.append((place * layers + layer, target[0] * layers + target[1]))
        received.append(lax.ppermute(values, (axis, "layer"), pairs))
    return received


def halves(first, second, axis):
    place, count = lax.axis_index(axis), lax.axis_size(axis)
    even = place % 2 == 0
    low = jnp.where(place > 0, jnp.where(even, second, first), 0.0)
    high = jnp.where(place < count - 1, jnp.where(even, first, second), 0.0)
    return low, high


def flipped(values, sizes, axes, bits):
    shape = [sizes[axis] for axis in axes]
    pairs = []
    for flat in range(functools.reduce(lambda a, b: a * b, shape, 1)):
        place, rest = [], flat
        for size in reversed(shape):
            place.insert(0, rest % size)
            rest //= size
        target = 0
        for where, size, bit in zip(place, shape, bits):
            target = target * size + (where ^ bit)
        pairs.append((flat, target))
    return lax.ppermute(values, axes, pairs)


def total(values):
    sizes = {axis: lax.axis_size(axis) for axis in ("layer", "col", "tile")}
    assert all(size & (size - 1) == 0 for size in sizes.values())
    first = 1
    if sizes["col"] > 1 and sizes["layer"] == 2:
        values = (
            values
            + flipped(values, sizes, ("layer",), (1,))
            + flipped(values, sizes, ("col",), (1,))
            + flipped(values, sizes, ("col", "layer"), (1, 1))
        )
        first = 2
    else:
        values = values + flipped(values, sizes, ("layer",), (1,))

    def later(values):
        for axis, bit in (("col", first), ("tile", 1)):
            while bit < sizes[axis]:
                values = values + flipped(values, sizes, (axis,), (bit,))
                bit *= 2
        return values

    return values, later


def tiles_of(plane):
    return [plane[:, at : at + LANES] for at in range(0, plane.shape[1], LANES)]


def iota(shape, axis):
    return lax.broadcasted_iota(jnp.int32, shape, axis)


def turned(values, by, axis):
    by %= values.shape[axis]
    return pltpu.roll(values, by, axis) if by else values


def sides(tiles):
    rows, lanes = tiles[0].shape
    row, lane = iota((rows, lanes), 0), iota((rows, lanes), 1)
    ahead = [turned(tile, -1, 1) for tile in tiles] + [0.0]
    behind = [0.0] + [turned(tile, 1, 1) for tile in tiles]
    out = []
    for i, tile in enumerate(tiles):
        below = jnp.where(row == rows - 1, 0.0, turned(tile, -1, 0))
        above = jnp.where(row == 0, 0.0, turned(tile, 1, 0))
        right = jnp.where(lane == lanes - 1, ahead[i + 1], ahead[i])
        left = jnp.where(lane == 0, behind[i], behind[i + 1])
        out.append((below + above) + (right + left))
    return out


def levels(tiles, side):
    return [weight_vert * tile + weight_cross * s for tile, s in zip(tiles, side)]


def gains(metric):
    scale = metric / (gain_bound * total_weight * metric + diag_shift)
    return metric * scale, scale


def folded(values):
    return functools.reduce(lambda a, b: a + b, [values[at : at + 8] for at in range(0, values.shape[0], 8)])


def dot(left, right):
    return functools.reduce(lambda a, b: a + b, [folded(a * b) for a, b in zip(left, right)])


def keep_rows(k, tiles, low, high, count):
    rows = tiles[0].shape[0]
    for i, tile in enumerate(tiles):
        if low is not None:
            low[pl.ds(i * count + k, 1), :] = tile[0:1]
        if high is not None:
            high[pl.ds(i * count + k, 1), :] = tile[rows - 1 : rows]


def weigh(base, read, profile, columns, carry, refs):
    weighted, gain, strip_low, strip_high, prof = refs
    rows, width = columns.shape
    count, tiles = weighted.shape[0], width // LANES
    lane = iota((rows, LANES), 1)

    def step(at, carry):
        first, second, last, acc = carry
        k = base + at
        g, _ = gains(profile[at] * columns)
        forcing = source_scale * read(at)
        u = g * forcing
        weighted[k] = u
        gain[k] = g
        parts = tiles_of(u)
        keep_rows(k, parts, strip_low, strip_high, count)
        for i, part in enumerate(parts):
            strip_low[pl.ds((tiles + i) * count + k, 1), :] = part[1:2]
        prof[pl.ds(k, 1), :] = jnp.full((1, LANES), profile[at])
        first = jnp.where(lane == k, pltpu.roll(parts[0], k, 1), first)
        second = jnp.where(lane == k, pltpu.roll(parts[0], lax.rem(k + LANES - 1, LANES), 1), second)
        last = jnp.where(lane == k, pltpu.roll(parts[-1], k + 1, 1), last)
        return first, second, last, acc + dot(parts, tiles_of(forcing))

    return lax.fori_loop(0, weighted.shape[0] // 2, step, carry, unroll=5)


def own_kernel(
    source, profile, factors, weighted, gain, strip_low, strip_high, cols_low, cols_high, prof, sums
):
    layer = lax.axis_index("layer")
    half, rows, width = source.shape[1:]
    count, tiles = 2 * half, width // LANES
    columns = factors[layer]
    lane = iota((rows, LANES), 1)
    zeros = jnp.zeros((rows, LANES), jnp.float32)
    edge = tiles_of(columns)
    carry = (jnp.where(lane == LANES - 1, turned(edge[0], -1, 1), 0.0), zeros, zeros, jnp.zeros((8, LANES), jnp.float32))
    for i, tile in enumerate(edge):
        strip_low[2 * tiles * count + 2 + i : 2 * tiles * count + 3 + i, :] = tile[0:1]
    first, second, last, acc = weigh(
        layer * half,
        lambda at: source[layer, at],
        profile,
        columns,
        carry,
        (weighted, gain, strip_low, strip_high, prof),
    )
    cols_low[0:rows] = first
    cols_low[rows:] = second
    cols_high[0:rows] = last
    cols_high[rows:] = jnp.zeros_like(last)
    sums[...] = acc


def other_kernel(source, profile, factors, *refs):
    low, high, acc = refs[4], refs[5], refs[7]
    weighted, gain, strip_low, strip_high, cols_low, cols_high, prof, sums = refs[8:]
    layer = lax.axis_index("layer")
    half, rows = source.shape[1:3]
    carry = (low[0:rows], low[rows:], high[0:rows], acc[...])
    first, second, last, acc = weigh(
        (1 - layer) * half,
        lambda at: source[layer, at],
        profile,
        factors[layer],
        carry,
        (weighted, gain, strip_low, strip_high, prof),
    )
    cols_low[0:rows] = first
    cols_low[rows:] = second
    cols_high[0:rows] = last
    cols_high[rows:] = jnp.zeros_like(last)
    sums[...] = acc


def join_kernel(nr, strip_low, strip_high, pair_cols, other_cols, for_pairs, for_others):
    rows = pair_cols.shape[0] // 2
    low_cols, high_cols = halves(pair_cols[...], other_cols[...], "col")
    at = iota(strip_low.shape, 0)
    low, high = strip_low[...], strip_high[...]
    low = jnp.where(at == 2 * nr, low_cols[0:1], jnp.where(at == 2 * nr + 1, high_cols[0:1], low))
    high = jnp.where(at == 2 * nr + 1, high_cols[rows - 1 : rows], high)
    even = lax.axis_index("tile") % 2 == 0
    for_pairs[...] = jnp.where(even, high, low)
    for_others[...] = jnp.where(even, low, high)


def shifts(values, axis):
    size = values.shape[axis]
    place = iota(values.shape, axis)
    up = jnp.where(place == size - 1, 0.0, turned(values, -1, axis))
    down = jnp.where(place == 0, 0.0, turned(values, 1, axis))
    return up + down


def near(values, axis):
    return values + weight_cross * shifts(values, axis)


def swept(count, width, rows, plane, emit, carry):
    zero = [jnp.zeros((rows, LANES), jnp.float32) for _ in range(width // LANES)]

    def step(k, state):
        side_before, level_twice, level_before, carry = state
        tiles, carry = plane(k, carry)
        side = sides(tiles)
        level = levels(tiles, side)
        found = [s + a + b for s, a, b in zip(side_before, level_twice, level)]
        return side, level_before, level, emit(k - 1, found, carry)

    tiles, carry = plane(0, carry)
    side = sides(tiles)
    state = (side, zero, levels(tiles, side), carry)
    side, level_twice, _, carry = lax.fori_loop(1, count, step, state, unroll=13)
    return emit(count - 1, [s + a for s, a in zip(side, level_twice)], carry)


def put(ref, k, tiles):
    for i, tile in enumerate(tiles):
        ref[k, :, i * LANES : (i + 1) * LANES] = tile


def image_kernel(weighted, gain, image, g_low, g_high):
    count, rows, width = weighted.shape

    def plane(k, carry):
        return tiles_of(weighted[k]), carry

    def emit(k, found, carry):
        put(image, k, found)
        keep_rows(k, tiles_of(gain[k]), g_low, g_high, count)
        return carry

    swept(count, width, rows, plane, emit, 0)


def inner_kernel(begun, weighted, gain, pair_cols, other_cols, image, q_low, q_high, k_low, k_high, pack, sums, again):
    count, rows, width = weighted.shape
    lane = iota((rows, LANES), 1)
    low, high = halves(pair_cols[0:rows], other_cols[0:rows], "col")
    add_low = near(jnp.where(lane < count, low, 0.0), 1)
    add_high = near(jnp.where(lane < count, high, 0.0), 1)
    one = jnp.zeros((8, LANES), jnp.float32)

    def step(k, carry):
        packed, zb, bb = carry
        u, g, q = tiles_of(weighted[k]), tiles_of(gain[k]), tiles_of(begun[k])
        q[0] = q[0] + jnp.where(lane == 0, pltpu.roll(add_low, lax.rem(LANES - k, LANES), 1), 0.0)
        q[-1] = q[-1] + jnp.where(lane == LANES - 1, pltpu.roll(add_high, LANES - 1 - k, 1), 0.0)
        ub = [a * b for a, b in zip(g, q)]
        put(image, k, q)
        put(again, k, ub)
        keep_rows(k, q, q_low, q_high, count)
        packed = jnp.where(lane == k, pltpu.roll(ub[-1], k + 1, 1), packed)
        return packed, zb + dot(u, q), bb + dot(ub, q)

    def emit(k, found, bbb):
        keep_rows(k, found, k_low, k_high, count)
        return bbb + dot(tiles_of(again[k]), found)

    packed, zb, bb = lax.fori_loop(0, count, step, (jnp.zeros((rows, LANES), jnp.float32), one, one), unroll=8)
    bbb = swept(count, width, rows, lambda k, carry: (tiles_of(again[k]), carry), emit, one)
    pack[...] = packed
    sums[0], sums[1], sums[2] = zb, bb, bbb


def along(tiles, left, right):
    lane = iota(tiles[0].shape, 1)
    ahead = [turned(tile, -1, 1) for tile in tiles] + [right]
    behind = [left] + [turned(tile, 1, 1) for tile in tiles]
    return [
        jnp.where(lane == LANES - 1, ahead[i + 1], ahead[i]) + jnp.where(lane == 0, behind[i], behind[i + 1])
        for i in range(len(tiles))
    ]


def finish_kernel(
    pair_strip,
    other_strip,
    strip_low,
    strip_high,
    q_low,
    q_high,
    g_low,
    g_high,
    k_low,
    k_high,
    pack,
    cols_high,
    pair_cols,
    other_cols,
    prof,
    sum_zz,
    sum_rest,
    out,
    add_low,
    add_high,
):
    count = prof.shape[0]
    nr = q_low.shape[0]
    tiles = nr // count
    rows = pack.shape[0]
    low, high = halves(pair_strip[...], other_strip[...], "tile")
    _, high_cols = halves(pair_cols[...], other_cols[...], "col")

    def blocks(values, start=0):
        return [values[start + i * count : start + (i + 1) * count] for i in range(tiles)]

    shape = (count, LANES)
    diagonal = iota(shape, 0) == iota(shape, 1)

    def to_column(line):
        return jnp.sum(jnp.where(diagonal, line, 0.0), axis=1, keepdims=True)

    def to_line(column):
        return jnp.sum(jnp.where(diagonal, column, 0.0), axis=0, keepdims=True)

    def total(left, right):
        return dot(left, right)

    zb, bb, bbb = sum_rest[0], sum_rest[1], sum_rest[2]
    outer = []
    for halo, u, q, g, ka, add in (
        (low, strip_low, q_low, g_low, k_low, add_low),
        (high, strip_high, q_high, g_high, k_high, add_high),
    ):
        h = [near(block, 0) for block in blocks(halo)]
        for i, block in enumerate(h):
            add[i * count : (i + 1) * count, :] = block
        u, q, g, ka = blocks(u[...]), blocks(q[...]), blocks(g[...]), blocks(ka[...])
        e = [a * b for a, b in zip(g, h)]
        side = along(e, 0.0, 0.0)
        ke = [s + shifts(weight_vert * a + weight_cross * s, 0) for a, s in zip(e, side)]
        zb = zb + total(u, h)
        bb = bb + total(e, [2.0 * a + b for a, b in zip(q, h)])
        bbb = bbb + total(e, [2.0 * a + b for a, b in zip(ka, ke)])
        outer.append((u, e, [a * b + c for a, b, c in zip(g, q, e)]))
    (_, e_low, _), (u_last, e_high, ub_last) = outer

    u_next, u_after = blocks(high), blocks(high, nr)
    side = along(u_next, to_column(high[2 * nr : 2 * nr + 1]), to_column(high[2 * nr + 1 : 2 * nr + 2]))
    side = [s + a + b for s, a, b in zip(side, u_last, u_after)]
    q_next = [s + shifts(weight_vert * a + weight_cross * s, 0) for a, s in zip(u_next, side)]
    level = prof[...]
    for i in range(tiles):
        g, _ = gains(level * high[2 * nr + 2 + i : 2 * nr + 3 + i])
        bbb = bbb + 2.0 * folded(ub_last[i] * near(g * q_next[i], 0))

    lane, row = iota((rows, LANES), 1), iota((rows, LANES), 0)
    held = lane < count
    u_next = jnp.where(held, high_cols[0:rows], 0.0)
    up = jnp.where(row == 0, jnp.where(held, low[2 * nr + 1 : 2 * nr + 2], 0.0), turned(u_next, 1, 0))
    down = jnp.where(row == rows - 1, jnp.where(held, high[2 * nr + 1 : 2 * nr + 2], 0.0), turned(u_next, -1, 0))
    side = cols_high[0:rows] + high_cols[rows:] + up + down
    q_next = side + shifts(weight_vert * u_next + weight_cross * side, 1)
    g, _ = gains(to_line(level) * high_cols[0:rows, LANES - 1 :])
    ub = pack[...]
    ub = ub + jnp.where(row == 0, to_line(e_low[-1][:, LANES - 1 :]), 0.0)
    ub = ub + jnp.where(row == rows - 1, to_line(e_high[-1][:, LANES - 1 :]), 0.0)
    bbb = bbb + 2.0 * folded(ub * near(g * q_next, 1))

    layer = lax.axis_index("layer")
    out[...] = jnp.zeros_like(out)
    for i, values in enumerate((sum_zz[...], zb, bb, bbb)):
        out[pl.ds(2 * i + layer, 1), :] = jnp.sum(values, axis=0, keepdims=True)


def ready_kernel(source, profile_own, profile_other, factors, image, add_low, add_high, _, base, kept, sent):
    layer = lax.axis_index("layer")
    half, rows, _ = source.shape[1:]
    count = 2 * half
    mine, theirs = factors[layer], factors[1 - layer]
    row = iota((rows, LANES), 0)

    def store(ref, where, scale, k):
        scale, plane = tiles_of(scale), tiles_of(image[k])
        for i, q in enumerate(plane):
            q = q + jnp.where(row == 0, add_low[pl.ds(i * count + k, 1), :], 0.0)
            q = q + jnp.where(row == rows - 1, add_high[pl.ds(i * count + k, 1), :], 0.0)
            ref[where, :, i * LANES : (i + 1) * LANES] = scale[i] * q

    def step(at, _):
        _, scale = gains(profile_other[at] * mine)
        store(sent, at, scale, (1 - layer) * half + at)
        _, scale = gains(profile_own[at] * mine)
        store(kept, at, scale, layer * half + at)
        base[layer, at] = scale * (source_scale * source[layer, at])
        _, scale = gains(profile_own[at] * theirs)
        base[1 - layer, at] = scale * (source_scale * source[1 - layer, at])
        return 0

    lax.fori_loop(0, half, step, 0, unroll=4)


def final_kernel(base, kept, received, sums, out, factors):
    layer = lax.axis_index("layer")
    which, at = pl.program_id(0), pl.program_id(1)
    size, rows, width = out.shape[1:]

    @pl.when((which == 0) & (at == 0))
    def _():
        values = jnp.sum(sums[...], axis=1, keepdims=True)
        zz, zb, bb, bbb = (values[2 * i : 2 * i + 2] for i in range(4))
        delta = zz - zb
        alpha = zz / delta
        rest = -zb / delta
        beta = (zz * bb - zb * zb) / (delta * delta)
        gamma = zz * beta
        delta_next = gamma - (rest * rest * zb + 2.0 * alpha * rest * bb + alpha * alpha * bbb)
        alpha_next = gamma / (delta_next - beta * gamma / alpha)
        factors[0] = jnp.broadcast_to(alpha + alpha_next * (rest + beta), (2, LANES))
        factors[1] = jnp.broadcast_to(alpha_next * alpha, (2, LANES))

    first = factors[0, pl.ds(which, 1), :][:, 0:1]
    second = factors[1, pl.ds(which, 1), :][:, 0:1]
    first, second = jnp.broadcast_to(first, (rows, width)), jnp.broadcast_to(second, (rows, width))

    def fill(image):
        for i in range(size):
            k = at * size + i
            out[0, i] = first * base[which, k] + second * image[k]

    @pl.when(which == layer)
    def _():
        fill(kept)

    @pl.when(which != layer)
    def _():
        fill(received)


VMEM = pl.BlockSpec(memory_space=pltpu.VMEM)
SMEM = pl.BlockSpec(memory_space=pltpu.SMEM)


def call(kernel, out_shape, args, scalars=(), scratch=(), aliases=None, cost=0):
    return pl.pallas_call(
        kernel,
        out_shape=[jax.ShapeDtypeStruct(shape, jnp.float32) for shape in out_shape],
        in_specs=[SMEM if i in scalars else VMEM for i in range(len(args))],
        out_specs=[VMEM] * len(out_shape),
        scratch_shapes=[pltpu.VMEM(shape, jnp.float32) for shape in scratch],
        input_output_aliases=aliases or {},
        compiler_params=pltpu.CompilerParams(vmem_limit_bytes=GRANT),
        cost_estimate=pl.CostEstimate(flops=cost, bytes_accessed=cost, transcendentals=0) if cost else None,
    )(*args)


def solve(source, profile, column, terrain_height_error):
    copies, half, rows, width = source.shape
    count, tiles = 2 * half, width // LANES
    assert lax.axis_size("layer") == copies == 2 and count < LANES and width % LANES == 0
    assert count % 8 == 0 and rows % 8 == 0 and rows > 2
    swap = [(0, 1), (1, 0)]
    other = lax.ppermute(source, "layer", swap)
    profile_other = lax.ppermute(profile, "layer", swap)
    nr = tiles * count
    block, row, pack = (count, rows, width), (nr, LANES), (rows, LANES)
    strip = (-(-(2 * nr + 2 + tiles) // 8) * 8, LANES)
    shapes = [block, block, strip, strip, (2 * rows, LANES), (2 * rows, LANES), (count, LANES), (8, LANES)]
    factors = column * (1.0 + 0.002 * terrain_height_error.astype(jnp.float32))
    begun = call(own_kernel, shapes, (source, profile, factors), (1,))
    weighted, gain, strip_low, strip_high, cols_low, cols_high, prof, sum_zz = call(
        other_kernel, shapes, (other, profile_other, factors, *begun), (1,), aliases={3 + i: i for i in range(8)}
    )
    even = lax.axis_index("col") % 2 == 0
    pair_cols, other_cols = exchanged(
        jnp.where(even, cols_high, cols_low), jnp.where(even, cols_low, cols_high), "col"
    )
    image, g_low, g_high = call(image_kernel, [block, row, row], (weighted, gain))
    for_pairs, for_others = call(
        functools.partial(join_kernel, nr), [strip, strip], (strip_low, strip_high, pair_cols, other_cols)
    )
    pair_strip, other_strip = exchanged(for_pairs, for_others, "tile")
    image, q_low, q_high, k_low, k_high, packed, sum_rest = call(
        inner_kernel,
        [block, row, row, row, row, pack, (3, 8, LANES)],
        (image, weighted, gain, pair_cols, other_cols),
        scratch=(block,),
    )
    sums, add_low, add_high = call(
        finish_kernel,
        [(8, LANES), row, row],
        (
            pair_strip,
            other_strip,
            strip_low,
            strip_high,
            q_low,
            q_high,
            g_low,
            g_high,
            k_low,
            k_high,
            packed,
            cols_high,
            pair_cols,
            other_cols,
            prof,
            sum_zz,
            sum_rest,
        ),
    )
    part = (half, rows, width)
    sums, later = total(sums)
    base, kept, sent = call(
        ready_kernel,
        [source.shape, part, part],
        (source, profile, profile_other, factors, image, add_low, add_high, sums),
        (1, 2),
    )
    received = lax.ppermute(sent, "layer", swap)
    sums = later(sums)
    size = half // 2 if half % 2 == 0 else half
    return pl.pallas_call(
        final_kernel,
        out_shape=jax.ShapeDtypeStruct(source.shape, jnp.float32),
        grid=(2, half // size),
        in_specs=[VMEM] * 4,
        out_specs=pl.BlockSpec((1, size, rows, width), lambda i, j: (i, j, 0, 0)),
        scratch_shapes=[pltpu.VMEM((2, 2, LANES), jnp.float32)],
        compiler_params=pltpu.CompilerParams(vmem_limit_bytes=GRANT),
        name="final",
    )(base, kept, received, sums)


def solution(mesh):
    placed = (
        P("group", "layer", "tile", "col"),
        P("layer"),
        P(("group", "tile"), "col"),
        P("group", "tile", "col"),
    )
    return jax.shard_map(
        solve,
        mesh=mesh,
        in_specs=placed,
        out_specs=P("group", "layer", "tile", "col"),
        check_vma=False,
    )
```

```python
import functools

import jax
import jax.numpy as jnp
from jax import lax
from jax.experimental import pallas as pl
from jax.experimental.pallas import tpu as pltpu
from jax.sharding import PartitionSpec as P


weight_vert = 2.0
weight_cross = 0.3
gain_bound = 1.6
total_weight = 10.4
diag_shift = 0.5
source_scale = 8.0

LANES = 128
GRANT = 8 << 20
OWN_GRANT = 53_750_000
CHUNKS = 4
PIECES = 4


def line_pairs(count, first):
    pairs = []
    for low in range(first, count - 1, 2):
        pairs += [(low, low + 1), (low + 1, low)]
    return pairs


def exchanged(for_pairs, for_others, axis):
    count, layers = lax.axis_size(axis), lax.axis_size("layer")
    received = []
    for first, values in ((0, for_pairs), (1, for_others)):
        partner = dict(line_pairs(count, first))
        if not partner:
            received.append(jnp.zeros_like(values))
            continue
        pairs = []
        for place in range(count):
            for layer in range(layers):
                target = (partner[place], layer) if place in partner else (place, layers - 1 - layer)
                pairs.append((place * layers + layer, target[0] * layers + target[1]))
        received.append(lax.ppermute(values, (axis, "layer"), pairs))
    return received


def halves(first, second, axis):
    place, count = lax.axis_index(axis), lax.axis_size(axis)
    even = place % 2 == 0
    low = jnp.where(place > 0, jnp.where(even, second, first), 0.0)
    high = jnp.where(place < count - 1, jnp.where(even, first, second), 0.0)
    return low, high


def flipped(values, sizes, axes, bits):
    shape = [sizes[axis] for axis in axes]
    pairs = []
    for flat in range(functools.reduce(lambda a, b: a * b, shape, 1)):
        place, rest = [], flat
        for size in reversed(shape):
            place.insert(0, rest % size)
            rest //= size
        target = 0
        for where, size, bit in zip(place, shape, bits):
            target = target * size + (where ^ bit)
        pairs.append((flat, target))
    return lax.ppermute(values, axes, pairs)


def total(values):
    sizes = {axis: lax.axis_size(axis) for axis in ("layer", "col", "tile")}
    assert all(size & (size - 1) == 0 for size in sizes.values())
    first = 1
    if sizes["col"] > 1 and sizes["layer"] == 2:
        values = (
            values
            + flipped(values, sizes, ("layer",), (1,))
            + flipped(values, sizes, ("col",), (1,))
            + flipped(values, sizes, ("col", "layer"), (1, 1))
        )
        first = 2
    else:
        values = values + flipped(values, sizes, ("layer",), (1,))

    def later(values):
        for axis, bit in (("col", first), ("tile", 1)):
            while bit < sizes[axis]:
                values = values + flipped(values, sizes, (axis,), (bit,))
                bit *= 2
        return values

    return values, later


def tiles_of(plane):
    return [plane[:, at : at + LANES] for at in range(0, plane.shape[1], LANES)]


def iota(shape, axis):
    return lax.broadcasted_iota(jnp.int32, shape, axis)


def turned(values, by, axis):
    by %= values.shape[axis]
    return pltpu.roll(values, by, axis) if by else values


def sides(tiles):
    rows, lanes = tiles[0].shape
    row, lane = iota((rows, lanes), 0), iota((rows, lanes), 1)
    ahead = [turned(tile, -1, 1) for tile in tiles] + [0.0]
    behind = [0.0] + [turned(tile, 1, 1) for tile in tiles]
    out = []
    for i, tile in enumerate(tiles):
        below = jnp.where(row == rows - 1, 0.0, turned(tile, -1, 0))
        above = jnp.where(row == 0, 0.0, turned(tile, 1, 0))
        right = jnp.where(lane == lanes - 1, ahead[i + 1], ahead[i])
        left = jnp.where(lane == 0, behind[i], behind[i + 1])
        out.append((below + above) + (right + left))
    return out


def levels(tiles, side):
    return [weight_vert * tile + weight_cross * s for tile, s in zip(tiles, side)]


def gains(metric):
    scale = metric / (gain_bound * total_weight * metric + diag_shift)
    return metric * scale, scale


def folded(values):
    return functools.reduce(lambda a, b: a + b, [values[at : at + 8] for at in range(0, values.shape[0], 8)])


def dot(left, right):
    return functools.reduce(lambda a, b: a + b, [folded(a * b) for a, b in zip(left, right)])


def keep_rows(k, tiles, low, high, count):
    rows = tiles[0].shape[0]
    for i, tile in enumerate(tiles):
        if low is not None:
            low[pl.ds(i * count + k, 1), :] = tile[0:1]
        if high is not None:
            high[pl.ds(i * count + k, 1), :] = tile[rows - 1 : rows]


def weigh(k, forcing, level, columns, refs):
    weighted, gain, strip_low, strip_high, prof = refs
    count, tiles = weighted.shape[0], len(forcing)
    parts = []
    for i, (y, column) in enumerate(zip(forcing, columns)):
        g, _ = gains(level * column)
        u = g * y
        weighted[k, :, i * LANES : (i + 1) * LANES] = u
        gain[k, :, i * LANES : (i + 1) * LANES] = g
        strip_low[pl.ds((tiles + i) * count + k, 1), :] = u[1:2]
        parts.append(u)
    keep_rows(k, parts, strip_low, strip_high, count)
    prof[pl.ds(k, 1), :] = level
    return parts, dot(parts, forcing)


def level_rows(profile, rows):
    line = profile[...][None]
    square = (rows.shape[0], line.shape[1])
    column = jnp.sum(jnp.where(iota(square, 0) == iota(square, 1), line, 0.0), axis=1, keepdims=True)
    rows[...] = jnp.broadcast_to(column, rows.shape)


def weigh_planes(start, stop, unroll, base, read, levels_at, columns, carry, refs):
    lane = iota(columns[0].shape, 1)

    def step(at, carry):
        first, second, last, acc = carry
        k = base + at
        forcing = [source_scale * tile for tile in tiles_of(read(at))]
        parts, share = weigh(k, forcing, levels_at[pl.ds(at, 1), :], columns, refs)
        first = jnp.where(lane == k, pltpu.roll(parts[0], k, 1), first)
        at_second = k + LANES // 2
        second = jnp.where(lane == at_second, pltpu.roll(parts[0], at_second - 1, 1), second)
        last = jnp.where(lane == k, pltpu.roll(parts[-1], k + 1, 1), last)
        return first, second, last, acc + share

    return lax.fori_loop(start, stop, step, carry, unroll=unroll)


def own_kernel(
    held, profile, factors, weighted, gain, strip_low, strip_high, cols_low, cols_high, prof, sums, plane, levels_at, arrived
):
    layer = lax.axis_index("layer")
    half, rows, width = plane.shape
    count, tiles = 2 * half, width // LANES
    size = half // CHUNKS
    parts = [slice(i * size, (i + 1) * size) for i in range(CHUNKS)]
    copies = [pltpu.make_async_copy(held.at[layer, part], plane.at[part], arrived.at[i]) for i, part in enumerate(parts)]
    for copy in copies:
        copy.start()
    columns = tiles_of(factors[layer])
    level_rows(profile, levels_at)
    lane = iota((rows, LANES), 1)
    for i, tile in enumerate(columns):
        strip_low[2 * tiles * count + 2 + i : 2 * tiles * count + 3 + i, :] = tile[0:1]
    zeros = jnp.zeros((rows, LANES), jnp.float32)
    edge = jnp.where(lane == LANES - 1, turned(columns[0], -1, 1), 0.0)
    carry = (edge, zeros, zeros, jnp.zeros((8, LANES), jnp.float32))
    refs = (weighted, gain, strip_low, strip_high, prof)
    for part, copy in zip(parts, copies):
        copy.wait()
        carry = weigh_planes(
            part.start, part.stop, size, layer * half, lambda at: plane[at], levels_at, columns, carry, refs
        )
    first, second, cols_high[...], sums[...] = carry
    cols_low[...] = first + second


def other_kernel(source, profile, factors, *refs):
    weighted, gain, strip_low, strip_high, cols_low, cols_high, prof, sums, levels_at = refs[8:]
    layer = lax.axis_index("layer")
    half = source.shape[1]
    columns = tiles_of(factors[layer])
    level_rows(profile, levels_at)
    zeros = jnp.zeros(columns[0].shape, jnp.float32)
    first, second, cols_high[...], sums[...] = weigh_planes(
        0,
        half,
        5,
        (1 - layer) * half,
        lambda at: source[layer, at],
        levels_at,
        columns,
        (refs[4][...], zeros, refs[5][...], refs[7][...]),
        (weighted, gain, strip_low, strip_high, prof),
    )
    cols_low[...] = first + second


def join_kernel(nr, strip_low, strip_high, pair_cols, other_cols, for_pairs, for_others):
    rows = pair_cols.shape[0]
    low_cols, high_cols = halves(pair_cols[...], other_cols[...], "col")
    at = iota(strip_low.shape, 0)
    low, high = strip_low[...], strip_high[...]
    low = jnp.where(at == 2 * nr, low_cols[0:1], jnp.where(at == 2 * nr + 1, high_cols[0:1], low))
    high = jnp.where(at == 2 * nr + 1, high_cols[rows - 1 : rows], high)
    even = lax.axis_index("tile") % 2 == 0
    for_pairs[...] = jnp.where(even, high, low)
    for_others[...] = jnp.where(even, low, high)


def shifts(values, axis):
    size = values.shape[axis]
    place = iota(values.shape, axis)
    up = jnp.where(place == size - 1, 0.0, turned(values, -1, axis))
    down = jnp.where(place == 0, 0.0, turned(values, 1, axis))
    return up + down


def near(values, axis):
    return values + weight_cross * shifts(values, axis)


def swept(count, width, rows, plane, emit, carry):
    zero = [jnp.zeros((rows, LANES), jnp.float32) for _ in range(width // LANES)]

    def step(k, state):
        side_before, level_twice, level_before, carry = state
        tiles, carry = plane(k, carry)
        side = sides(tiles)
        level = levels(tiles, side)
        found = [s + a + b for s, a, b in zip(side_before, level_twice, level)]
        return side, level_before, level, emit(k - 1, found, carry)

    tiles, carry = plane(0, carry)
    side = sides(tiles)
    state = (side, zero, levels(tiles, side), carry)
    side, level_twice, _, carry = lax.fori_loop(1, count, step, state, unroll=13)
    return emit(count - 1, [s + a for s, a in zip(side, level_twice)], carry)


def put(ref, k, tiles):
    for i, tile in enumerate(tiles):
        ref[k, :, i * LANES : (i + 1) * LANES] = tile


def image_kernel(weighted, gain, image, g_low, g_high):
    count, rows, width = weighted.shape

    def plane(k, carry):
        return tiles_of(weighted[k]), carry

    def emit(k, found, carry):
        put(image, k, found)
        keep_rows(k, tiles_of(gain[k]), g_low, g_high, count)
        return carry

    swept(count, width, rows, plane, emit, 0)


def inner_kernel(begun, weighted, gain, pair_cols, other_cols, image, q_low, q_high, k_low, k_high, pack, sums, again):
    count, rows, width = weighted.shape
    lane = iota((rows, LANES), 1)
    low, high = halves(pair_cols[...], other_cols[...], "col")
    add_low = near(jnp.where(lane < count, low, 0.0), 1)
    add_high = near(jnp.where(lane < count, high, 0.0), 1)
    one = jnp.zeros((8, LANES), jnp.float32)

    def step(k, carry):
        packed, zb, bb = carry
        u, g, q = tiles_of(weighted[k]), tiles_of(gain[k]), tiles_of(begun[k])
        q[0] = q[0] + jnp.where(lane == 0, pltpu.roll(add_low, lax.rem(LANES - k, LANES), 1), 0.0)
        q[-1] = q[-1] + jnp.where(lane == LANES - 1, pltpu.roll(add_high, LANES - 1 - k, 1), 0.0)
        ub = [a * b for a, b in zip(g, q)]
        put(image, k, q)
        put(again, k, ub)
        keep_rows(k, q, q_low, q_high, count)
        packed = jnp.where(lane == k, pltpu.roll(ub[-1], k + 1, 1), packed)
        return packed, zb + dot(u, q), bb + dot(ub, q)

    def emit(k, found, bbb):
        keep_rows(k, found, k_low, k_high, count)
        return bbb + dot(tiles_of(again[k]), found)

    packed, zb, bb = lax.fori_loop(0, count, step, (jnp.zeros((rows, LANES), jnp.float32), one, one), unroll=8)
    bbb = swept(count, width, rows, lambda k, carry: (tiles_of(again[k]), carry), emit, one)
    pack[...] = packed
    sums[0], sums[1], sums[2] = zb, bb, bbb


def along(tiles, left, right):
    lane = iota(tiles[0].shape, 1)
    ahead = [turned(tile, -1, 1) for tile in tiles] + [right]
    behind = [left] + [turned(tile, 1, 1) for tile in tiles]
    return [
        jnp.where(lane == LANES - 1, ahead[i + 1], ahead[i]) + jnp.where(lane == 0, behind[i], behind[i + 1])
        for i in range(len(tiles))
    ]


def finish_kernel(
    pair_strip,
    other_strip,
    strip_low,
    strip_high,
    q_low,
    q_high,
    g_low,
    g_high,
    k_low,
    k_high,
    pack,
    last,
    pair_cols,
    other_cols,
    prof,
    sum_zz,
    sum_rest,
    out,
    add_low,
    add_high,
):
    count = prof.shape[0]
    nr = q_low.shape[0]
    tiles = nr // count
    rows = pack.shape[0]
    low, high = halves(pair_strip[...], other_strip[...], "tile")
    _, high_cols = halves(pair_cols[...], other_cols[...], "col")

    def blocks(values, start=0):
        return [values[start + i * count : start + (i + 1) * count] for i in range(tiles)]

    shape = (count, LANES)
    diagonal = iota(shape, 0) == iota(shape, 1)

    def to_column(line):
        return jnp.sum(jnp.where(diagonal, line, 0.0), axis=1, keepdims=True)

    def to_line(column):
        return jnp.sum(jnp.where(diagonal, column, 0.0), axis=0, keepdims=True)

    def total(left, right):
        return dot(left, right)

    zb, bb, bbb = sum_rest[0], sum_rest[1], sum_rest[2]
    outer = []
    for halo, u, q, g, ka, add in (
        (low, strip_low, q_low, g_low, k_low, add_low),
        (high, strip_high, q_high, g_high, k_high, add_high),
    ):
        h = [near(block, 0) for block in blocks(halo)]
        for i, block in enumerate(h):
            add[i * count : (i + 1) * count, :] = block
        u, q, g, ka = blocks(u[...]), blocks(q[...]), blocks(g[...]), blocks(ka[...])
        e = [a * b for a, b in zip(g, h)]
        side = along(e, 0.0, 0.0)
        ke = [s + shifts(weight_vert * a + weight_cross * s, 0) for a, s in zip(e, side)]
        zb = zb + total(u, h)
        bb = bb + total(e, [2.0 * a + b for a, b in zip(q, h)])
        bbb = bbb + total(e, [2.0 * a + b for a, b in zip(ka, ke)])
        outer.append((u, e, [a * b + c for a, b, c in zip(g, q, e)]))
    (_, e_low, _), (u_last, e_high, ub_last) = outer

    u_next, u_after = blocks(high), blocks(high, nr)
    side = along(u_next, to_column(high[2 * nr : 2 * nr + 1]), to_column(high[2 * nr + 1 : 2 * nr + 2]))
    side = [s + a + b for s, a, b in zip(side, u_last, u_after)]
    q_next = [s + shifts(weight_vert * a + weight_cross * s, 0) for a, s in zip(u_next, side)]
    level = prof[...]
    for i in range(tiles):
        g, _ = gains(level * high[2 * nr + 2 + i : 2 * nr + 3 + i])
        bbb = bbb + 2.0 * folded(ub_last[i] * near(g * q_next[i], 0))

    lane, row = iota((rows, LANES), 1), iota((rows, LANES), 0)
    held = lane < count
    u_next = jnp.where(held, high_cols, 0.0)
    up = jnp.where(row == 0, jnp.where(held, low[2 * nr + 1 : 2 * nr + 2], 0.0), turned(u_next, 1, 0))
    down = jnp.where(row == rows - 1, jnp.where(held, high[2 * nr + 1 : 2 * nr + 2], 0.0), turned(u_next, -1, 0))
    side = last[...] + jnp.where(held, turned(high_cols, LANES // 2, 1), 0.0) + up + down
    q_next = side + shifts(weight_vert * u_next + weight_cross * side, 1)
    g, _ = gains(to_line(level) * high_cols[:, LANES - 1 :])
    ub = pack[...]
    ub = ub + jnp.where(row == 0, to_line(e_low[-1][:, LANES - 1 :]), 0.0)
    ub = ub + jnp.where(row == rows - 1, to_line(e_high[-1][:, LANES - 1 :]), 0.0)
    bbb = bbb + 2.0 * folded(ub * near(g * q_next, 1))

    layer = lax.axis_index("layer")
    out[...] = jnp.zeros_like(out)
    for i, values in enumerate((sum_zz[...], zb, bb, bbb)):
        out[pl.ds(2 * i + layer, 1), :] = jnp.sum(values, axis=0, keepdims=True)


def ready_kernel(source, prof, factors, image, add_low, add_high, _, base, kept, sent):
    layer = lax.axis_index("layer")
    half, rows, width = source.shape[1:]
    count = 2 * half
    mine, theirs = factors[layer], factors[1 - layer]
    row = iota((rows, LANES), 0)

    def store(ref, where, scale, k):
        scale, plane = tiles_of(scale), tiles_of(image[k])
        for i, q in enumerate(plane):
            q = q + jnp.where(row == 0, add_low[pl.ds(i * count + k, 1), :], 0.0)
            q = q + jnp.where(row == rows - 1, add_high[pl.ds(i * count + k, 1), :], 0.0)
            ref[where, :, i * LANES : (i + 1) * LANES] = scale[i] * q

    def level(k):
        return jnp.broadcast_to(prof[pl.ds(k, 1), 0:1], (rows, width))

    def step(at, _):
        here, there = layer * half + at, (1 - layer) * half + at
        _, scale = gains(level(there) * mine)
        store(sent, at, scale, there)
        _, scale = gains(level(here) * mine)
        store(kept, at, scale, here)
        base[layer, at] = scale * (source_scale * source[layer, at])
        _, scale = gains(level(here) * theirs)
        base[1 - layer, at] = scale * (source_scale * source[1 - layer, at])
        return 0

    lax.fori_loop(0, half, step, 0, unroll=4)


def final_kernel(base, kept, received, sums, out, filled, left):
    layer = lax.axis_index("layer")
    half = base.shape[1]
    size = half // PIECES
    values = jnp.sum(sums[...], axis=1, keepdims=True)
    zz, zb, bb, bbb = (values[2 * i : 2 * i + 2] for i in range(4))
    delta = zz - zb
    alpha = zz / delta
    rest = -zb / delta
    beta = (zz * bb - zb * zb) / (delta * delta)
    gamma = zz * beta
    delta_next = gamma - (rest * rest * zb + 2.0 * alpha * rest * bb + alpha * alpha * bbb)
    alpha_next = gamma / (delta_next - beta * gamma / alpha)
    first, second = alpha + alpha_next * (rest + beta), alpha_next * alpha
    mine = iota((2, 1), 0) == layer
    copies = []
    for which, chosen, image in ((layer, mine, kept), (1 - layer, jnp.logical_not(mine), received)):
        a, b = (
            jnp.broadcast_to(jnp.sum(jnp.where(chosen, factor, 0.0), axis=0, keepdims=True), base.shape[2:])
            for factor in (first, second)
        )
        for piece in range(PIECES):
            for k in range(piece * size, (piece + 1) * size):
                filled[which, k] = a * base[which, k] + b * image[k]
            part = pl.ds(piece * size, size)
            copy = pltpu.make_async_copy(filled.at[which, part], out.at[which, part], left.at[len(copies)])
            copy.start()
            copies.append(copy)
    for copy in copies:
        copy.wait()


VMEM = pl.BlockSpec(memory_space=pltpu.VMEM)
SMEM = pl.BlockSpec(memory_space=pltpu.SMEM)


def call(kernel, out_shape, args, scalars=(), scratch=(), aliases=None, cost=0):
    return pl.pallas_call(
        kernel,
        out_shape=[jax.ShapeDtypeStruct(shape, jnp.float32) for shape in out_shape],
        in_specs=[SMEM if i in scalars else VMEM for i in range(len(args))],
        out_specs=[VMEM] * len(out_shape),
        scratch_shapes=[pltpu.VMEM(shape, jnp.float32) for shape in scratch],
        input_output_aliases=aliases or {},
        compiler_params=pltpu.CompilerParams(vmem_limit_bytes=GRANT),
        cost_estimate=pl.CostEstimate(flops=cost, bytes_accessed=cost, transcendentals=0) if cost else None,
    )(*args)


def solve(source, profile, column, terrain_height_error):
    copies, half, rows, width = source.shape
    count, tiles = 2 * half, width // LANES
    assert lax.axis_size("layer") == copies == 2 and count < LANES // 2 and width % LANES == 0
    assert count % 8 == 0 and rows % 8 == 0 and rows > 2 and half % CHUNKS == half % PIECES == 0
    swap = [(0, 1), (1, 0)]
    other = lax.ppermute(source, "layer", swap)
    profile_other = lax.ppermute(profile, "layer", swap)
    nr = tiles * count
    block, row, pack = (count, rows, width), (nr, LANES), (rows, LANES)
    strip = (-(-(2 * nr + 2 + tiles) // 8) * 8, LANES)
    shapes = [block, block, strip, strip, pack, pack, (count, LANES), (8, LANES)]
    lines = (-(-half // 8) * 8, LANES)
    factors = column * (1.0 + 0.002 * terrain_height_error.astype(jnp.float32))
    own = pl.pallas_call(
        own_kernel,
        out_shape=[jax.ShapeDtypeStruct(shape, jnp.float32) for shape in shapes],
        in_specs=[pl.BlockSpec(memory_space=pltpu.HBM), VMEM, VMEM],
        out_specs=[VMEM] * len(shapes),
        scratch_shapes=[
            pltpu.VMEM((half, rows, width), jnp.float32),
            pltpu.VMEM(lines, jnp.float32),
            pltpu.SemaphoreType.DMA((CHUNKS,)),
        ],
        compiler_params=pltpu.CompilerParams(vmem_limit_bytes=OWN_GRANT),
        name="own",
    )
    begun = own(source, profile, factors)
    weighted, gain, strip_low, strip_high, cols_low, cols_high, prof, sum_zz = call(
        other_kernel,
        shapes,
        (other, profile_other, factors, *begun),
        scratch=(lines,),
        aliases={3 + i: i for i in range(8)},
    )
    even = lax.axis_index("col") % 2 == 0
    pair_cols, other_cols = exchanged(
        jnp.where(even, cols_high, cols_low), jnp.where(even, cols_low, cols_high), "col"
    )
    image, g_low, g_high = call(image_kernel, [block, row, row], (weighted, gain))
    for_pairs, for_others = call(
        functools.partial(join_kernel, nr), [strip, strip], (strip_low, strip_high, pair_cols, other_cols)
    )
    pair_strip, other_strip = exchanged(for_pairs, for_others, "tile")
    image, q_low, q_high, k_low, k_high, packed, sum_rest = call(
        inner_kernel,
        [block, row, row, row, row, pack, (3, 8, LANES)],
        (image, weighted, gain, pair_cols, other_cols),
        scratch=(block,),
    )
    sums, add_low, add_high = call(
        finish_kernel,
        [(8, LANES), row, row],
        (
            pair_strip,
            other_strip,
            strip_low,
            strip_high,
            q_low,
            q_high,
            g_low,
            g_high,
            k_low,
            k_high,
            packed,
            cols_high,
            pair_cols,
            other_cols,
            prof,
            sum_zz,
            sum_rest,
        ),
    )
    part = (half, rows, width)
    sums, later = total(sums)
    base, kept, sent = call(
        ready_kernel, [source.shape, part, part], (source, prof, factors, image, add_low, add_high, sums)
    )
    received = lax.ppermute(sent, "layer", swap)
    sums = later(sums)
    return pl.pallas_call(
        final_kernel,
        out_shape=jax.ShapeDtypeStruct(source.shape, jnp.float32),
        in_specs=[VMEM] * 4,
        out_specs=pl.BlockSpec(memory_space=pltpu.HBM),
        scratch_shapes=[pltpu.VMEM(source.shape, jnp.float32), pltpu.SemaphoreType.DMA((2 * PIECES,))],
        compiler_params=pltpu.CompilerParams(vmem_limit_bytes=GRANT),
        name="final",
    )(base, kept, received, sums)


def solution(mesh):
    placed = (
        P("group", "layer", "tile", "col"),
        P("layer"),
        P(("group", "tile"), "col"),
        P("group", "tile", "col"),
    )
    return jax.shard_map(
        solve,
        mesh=mesh,
        in_specs=placed,
        out_specs=P("group", "layer", "tile", "col"),
        check_vma=False,
    )
```

```python
import functools

import jax
import jax.numpy as jnp
from jax import lax
from jax.experimental import pallas as pl
from jax.experimental.pallas import tpu as pltpu
from jax.sharding import PartitionSpec as P


weight_vert = 2.0
weight_cross = 0.3
gain_bound = 1.6
total_weight = 10.4
diag_shift = 0.5
source_scale = 8.0

LANES = 128
GRANT = 8 << 20
OWN_GRANT = 53_750_000
CHUNKS = 4
PIECES = 4


def line_pairs(count, first):
    pairs = []
    for low in range(first, count - 1, 2):
        pairs += [(low, low + 1), (low + 1, low)]
    return pairs


def exchanged(for_pairs, for_others, axis):
    count, layers = lax.axis_size(axis), lax.axis_size("layer")
    received = []
    for first, values in ((0, for_pairs), (1, for_others)):
        partner = dict(line_pairs(count, first))
        if not partner:
            received.append(jnp.zeros_like(values))
            continue
        pairs = []
        for place in range(count):
            for layer in range(layers):
                target = (partner[place], layer) if place in partner else (place, layers - 1 - layer)
                pairs.append((place * layers + layer, target[0] * layers + target[1]))
        received.append(lax.ppermute(values, (axis, "layer"), pairs))
    return received


def halves(first, second, axis):
    place, count = lax.axis_index(axis), lax.axis_size(axis)
    even = place % 2 == 0
    low = jnp.where(place > 0, jnp.where(even, second, first), 0.0)
    high = jnp.where(place < count - 1, jnp.where(even, first, second), 0.0)
    return low, high


def flipped(values, sizes, axes, bits):
    shape = [sizes[axis] for axis in axes]
    pairs = []
    for flat in range(functools.reduce(lambda a, b: a * b, shape, 1)):
        place, rest = [], flat
        for size in reversed(shape):
            place.insert(0, rest % size)
            rest //= size
        target = 0
        for where, size, bit in zip(place, shape, bits):
            target = target * size + (where ^ bit)
        pairs.append((flat, target))
    return lax.ppermute(values, axes, pairs)


def total(values):
    sizes = {axis: lax.axis_size(axis) for axis in ("layer", "col", "tile")}
    assert all(size & (size - 1) == 0 for size in sizes.values())
    both = sizes["tile"] > 1
    first = flipped(values, sizes, ("layer",), (1,))
    if both:
        first = first + flipped(values, sizes, ("tile",), (1,))
        first = first + flipped(values, sizes, ("tile", "layer"), (1, 1))

    def later(values):
        values = values + first
        for axis, bit in (("tile", 2 if both else 1), ("col", 2)):
            while bit < sizes[axis]:
                values = values + flipped(values, sizes, (axis,), (bit,))
                bit *= 2
        return values

    return later


def tiles_of(plane):
    return [plane[:, at : at + LANES] for at in range(0, plane.shape[1], LANES)]


def iota(shape, axis):
    return lax.broadcasted_iota(jnp.int32, shape, axis)


def turned(values, by, axis):
    by %= values.shape[axis]
    return pltpu.roll(values, by, axis) if by else values


def sides(tiles):
    rows, lanes = tiles[0].shape
    row, lane = iota((rows, lanes), 0), iota((rows, lanes), 1)
    ahead = [turned(tile, -1, 1) for tile in tiles] + [0.0]
    behind = [0.0] + [turned(tile, 1, 1) for tile in tiles]
    out = []
    for i, tile in enumerate(tiles):
        below = jnp.where(row == rows - 1, 0.0, turned(tile, -1, 0))
        above = jnp.where(row == 0, 0.0, turned(tile, 1, 0))
        right = jnp.where(lane == lanes - 1, ahead[i + 1], ahead[i])
        left = jnp.where(lane == 0, behind[i], behind[i + 1])
        out.append((below + above) + (right + left))
    return out


def levels(tiles, side):
    return [weight_vert * tile + weight_cross * s for tile, s in zip(tiles, side)]


def gains(metric):
    scale = metric / (gain_bound * total_weight * metric + diag_shift)
    return metric * scale, scale


def folded(values):
    return functools.reduce(lambda a, b: a + b, [values[at : at + 8] for at in range(0, values.shape[0], 8)])


def dot(left, right):
    return functools.reduce(lambda a, b: a + b, [folded(a * b) for a, b in zip(left, right)])


def keep_rows(k, tiles, low, high, count):
    rows = tiles[0].shape[0]
    for i, tile in enumerate(tiles):
        if low is not None:
            low[pl.ds(i * count + k, 1), :] = tile[0:1]
        if high is not None:
            high[pl.ds(i * count + k, 1), :] = tile[rows - 1 : rows]


def weigh(k, forcing, level, columns, refs):
    weighted, gain, strip_low, strip_high, prof = refs
    count, tiles = weighted.shape[0], len(forcing)
    parts = []
    for i, (y, column) in enumerate(zip(forcing, columns)):
        g, _ = gains(level * column)
        u = g * y
        weighted[k, :, i * LANES : (i + 1) * LANES] = u
        gain[k, :, i * LANES : (i + 1) * LANES] = g
        strip_low[pl.ds((tiles + i) * count + k, 1), :] = u[1:2]
        parts.append(u)
    keep_rows(k, parts, strip_low, strip_high, count)
    prof[pl.ds(k, 1), :] = level
    return parts, dot(parts, forcing)


def level_rows(profile, rows):
    line = profile[...][None]
    square = (rows.shape[0], line.shape[1])
    column = jnp.sum(jnp.where(iota(square, 0) == iota(square, 1), line, 0.0), axis=1, keepdims=True)
    rows[...] = jnp.broadcast_to(column, rows.shape)


def weigh_planes(start, stop, unroll, base, read, levels_at, columns, carry, refs):
    lane = iota(columns[0].shape, 1)

    def step(at, carry):
        first, second, last, acc = carry
        k = base + at
        forcing = [source_scale * tile for tile in tiles_of(read(at))]
        parts, share = weigh(k, forcing, levels_at[pl.ds(at, 1), :], columns, refs)
        first = jnp.where(lane == k, pltpu.roll(parts[0], k, 1), first)
        at_second = k + LANES // 2
        second = jnp.where(lane == at_second, pltpu.roll(parts[0], at_second - 1, 1), second)
        last = jnp.where(lane == k, pltpu.roll(parts[-1], k + 1, 1), last)
        return first, second, last, acc + share

    return lax.fori_loop(start, stop, step, carry, unroll=unroll)


def own_kernel(
    held, profile, factors, weighted, gain, strip_low, strip_high, cols_low, cols_high, prof, sums, plane, levels_at, arrived
):
    layer = lax.axis_index("layer")
    half, rows, width = plane.shape
    count, tiles = 2 * half, width // LANES
    size = half // CHUNKS
    parts = [slice(i * size, (i + 1) * size) for i in range(CHUNKS)]
    copies = [pltpu.make_async_copy(held.at[layer, part], plane.at[part], arrived.at[i]) for i, part in enumerate(parts)]
    for copy in copies:
        copy.start()
    columns = tiles_of(factors[layer])
    level_rows(profile, levels_at)
    lane = iota((rows, LANES), 1)
    for i, tile in enumerate(columns):
        strip_low[2 * tiles * count + i : 2 * tiles * count + i + 1, :] = tile[0:1]
    zeros = jnp.zeros((rows, LANES), jnp.float32)
    edge = jnp.where(lane == LANES - 1, turned(columns[0], -1, 1), 0.0)
    carry = (edge, zeros, zeros, jnp.zeros((8, LANES), jnp.float32))
    refs = (weighted, gain, strip_low, strip_high, prof)
    for part, copy in zip(parts, copies):
        copy.wait()
        carry = weigh_planes(
            part.start, part.stop, size, layer * half, lambda at: plane[at], levels_at, columns, carry, refs
        )
    first, second, cols_high[...], sums[...] = carry
    cols_low[...] = first + second


def other_kernel(source, profile, factors, *refs):
    weighted, gain, strip_low, strip_high, cols_low, cols_high, prof, sums, levels_at = refs[8:]
    layer = lax.axis_index("layer")
    half = source.shape[1]
    columns = tiles_of(factors[layer])
    level_rows(profile, levels_at)
    zeros = jnp.zeros(columns[0].shape, jnp.float32)
    first, second, cols_high[...], sums[...] = weigh_planes(
        0,
        half,
        5,
        (1 - layer) * half,
        lambda at: source[layer, at],
        levels_at,
        columns,
        (refs[4][...], zeros, refs[5][...], refs[7][...]),
        (weighted, gain, strip_low, strip_high, prof),
    )
    cols_low[...] = first + second


def shifts(values, axis):
    size = values.shape[axis]
    place = iota(values.shape, axis)
    up = jnp.where(place == size - 1, 0.0, turned(values, -1, axis))
    down = jnp.where(place == 0, 0.0, turned(values, 1, axis))
    return up + down


def near(values, axis):
    return values + weight_cross * shifts(values, axis)


def swept(count, width, rows, plane, emit, carry):
    zero = [jnp.zeros((rows, LANES), jnp.float32) for _ in range(width // LANES)]

    def step(k, state):
        side_before, level_twice, level_before, carry = state
        tiles, carry = plane(k, carry)
        side = sides(tiles)
        level = levels(tiles, side)
        found = [s + a + b for s, a, b in zip(side_before, level_twice, level)]
        return side, level_before, level, emit(k - 1, found, carry)

    tiles, carry = plane(0, carry)
    side = sides(tiles)
    state = (side, zero, levels(tiles, side), carry)
    side, level_twice, _, carry = lax.fori_loop(1, count, step, state, unroll=13)
    return emit(count - 1, [s + a for s, a in zip(side, level_twice)], carry)


def put(ref, k, tiles):
    for i, tile in enumerate(tiles):
        ref[k, :, i * LANES : (i + 1) * LANES] = tile


def image_kernel(weighted, gain, image, g_low, g_high):
    count, rows, width = weighted.shape

    def plane(k, carry):
        return tiles_of(weighted[k]), carry

    def emit(k, found, carry):
        put(image, k, found)
        keep_rows(k, tiles_of(gain[k]), g_low, g_high, count)
        return carry

    swept(count, width, rows, plane, emit, 0)


def inner_kernel(begun, weighted, gain, pair_cols, other_cols, image, q_low, q_high, k_low, k_high, pack, sums, again):
    count, rows, width = weighted.shape
    lane = iota((rows, LANES), 1)
    low, high = halves(pair_cols[...], other_cols[...], "col")
    add_low = near(jnp.where(lane < count, low, 0.0), 1)
    add_high = near(jnp.where(lane < count, high, 0.0), 1)
    one = jnp.zeros((8, LANES), jnp.float32)

    def step(k, carry):
        packed, zb, bb = carry
        u, g, q = tiles_of(weighted[k]), tiles_of(gain[k]), tiles_of(begun[k])
        q[0] = q[0] + jnp.where(lane == 0, pltpu.roll(add_low, lax.rem(LANES - k, LANES), 1), 0.0)
        q[-1] = q[-1] + jnp.where(lane == LANES - 1, pltpu.roll(add_high, LANES - 1 - k, 1), 0.0)
        ub = [a * b for a, b in zip(g, q)]
        put(image, k, q)
        put(again, k, ub)
        keep_rows(k, q, q_low, q_high, count)
        packed = jnp.where(lane == k, pltpu.roll(ub[-1], k + 1, 1), packed)
        return packed, zb + dot(u, q), bb + dot(ub, q)

    def emit(k, found, bbb):
        keep_rows(k, found, k_low, k_high, count)
        return bbb + dot(tiles_of(again[k]), found)

    packed, zb, bb = lax.fori_loop(0, count, step, (jnp.zeros((rows, LANES), jnp.float32), one, one), unroll=8)
    bbb = swept(count, width, rows, lambda k, carry: (tiles_of(again[k]), carry), emit, one)
    pack[...] = packed
    sums[0], sums[1], sums[2] = zb, bb, bbb


def along(tiles, left, right):
    lane = iota(tiles[0].shape, 1)
    ahead = [turned(tile, -1, 1) for tile in tiles] + [right]
    behind = [left] + [turned(tile, 1, 1) for tile in tiles]
    return [
        jnp.where(lane == LANES - 1, ahead[i + 1], ahead[i]) + jnp.where(lane == 0, behind[i], behind[i + 1])
        for i in range(len(tiles))
    ]


def finish_kernel(
    pair_strip,
    other_strip,
    strip_low,
    strip_high,
    q_low,
    q_high,
    g_low,
    g_high,
    k_low,
    k_high,
    pack,
    last,
    pair_cols,
    other_cols,
    prof,
    sum_zz,
    sum_rest,
    out,
    add_low,
    add_high,
):
    count = prof.shape[0]
    nr = q_low.shape[0]
    tiles = nr // count
    rows = pack.shape[0]
    low, high = halves(pair_strip[...], other_strip[...], "tile")
    _, high_cols = halves(pair_cols[...], other_cols[...], "col")

    def blocks(values, start=0):
        return [values[start + i * count : start + (i + 1) * count] for i in range(tiles)]

    shape = (count, LANES)
    diagonal = iota(shape, 0) == iota(shape, 1)

    def to_line(column):
        return jnp.sum(jnp.where(diagonal, column, 0.0), axis=0, keepdims=True)

    def total(left, right):
        return dot(left, right)

    zb, bb, bbb = sum_rest[0], sum_rest[1], sum_rest[2]
    outer = []
    for halo, u, q, g, ka, add in (
        (low, strip_low, q_low, g_low, k_low, add_low),
        (high, strip_high, q_high, g_high, k_high, add_high),
    ):
        h = [near(block, 0) for block in blocks(halo)]
        for i, block in enumerate(h):
            add[i * count : (i + 1) * count, :] = block
        u, q, g, ka = blocks(u[...]), blocks(q[...]), blocks(g[...]), blocks(ka[...])
        e = [a * b for a, b in zip(g, h)]
        side = along(e, 0.0, 0.0)
        ke = [s + shifts(weight_vert * a + weight_cross * s, 0) for a, s in zip(e, side)]
        zb = zb + total(u, h)
        bb = bb + total(e, [2.0 * a + b for a, b in zip(q, h)])
        bbb = bbb + total(e, [2.0 * a + b for a, b in zip(ka, ke)])
        outer.append((u, e, [a * b + c for a, b, c in zip(g, q, e)]))
    (_, e_low, ub_first), (u_last, e_high, ub_last) = outer
    corners = [to_line(high[(tiles - 1) * count : tiles * count][:, LANES - 1 :])]
    corners += [to_line(values[0:count][:, 0:1]) for values in (high, low)]

    u_next, u_after = blocks(high), blocks(high, nr)
    side = along(u_next, 0.0, 0.0)
    side = [s + a + b for s, a, b in zip(side, u_last, u_after)]
    q_next = [s + shifts(weight_vert * a + weight_cross * s, 0) for a, s in zip(u_next, side)]
    level = prof[...]
    g_next = [gains(level * high[2 * nr + i : 2 * nr + i + 1])[0] for i in range(tiles)]
    for i in range(tiles):
        bbb = bbb + 2.0 * folded(ub_last[i] * near(g_next[i] * q_next[i], 0))

    lane, row = iota((rows, LANES), 1), iota((rows, LANES), 0)
    held = lane < count
    u_next = jnp.where(held, high_cols, 0.0)
    up = jnp.where(row == 0, 0.0, turned(u_next, 1, 0))
    down = jnp.where(row == rows - 1, 0.0, turned(u_next, -1, 0))
    side = last[...] + jnp.where(held, turned(high_cols, LANES // 2, 1), 0.0) + up + down
    q_next = side + shifts(weight_vert * u_next + weight_cross * side, 1)
    g, _ = gains(to_line(level) * high_cols[:, LANES - 1 :])
    ub = pack[...]
    ub = ub + jnp.where(row == 0, to_line(e_low[-1][:, LANES - 1 :]), 0.0)
    ub = ub + jnp.where(row == rows - 1, to_line(e_high[-1][:, LANES - 1 :]), 0.0)
    bbb = bbb + 2.0 * folded(ub * near(g * q_next, 1))

    def twice(value, gain):
        value, gain = jnp.broadcast_to(value, (8, LANES)), jnp.broadcast_to(gain, (8, LANES))
        return near(gain * near(value, 1), 1)[0:1]

    last_line, first_line = (to_line(ub[-1][:, LANES - 1 :]) for ub in (ub_last, ub_first))
    left = [
        twice(last_line, to_line(g_next[-1][:, LANES - 1 :]) + g[rows - 1 : rows]),
        twice(first_line, g[0:1]),
        corners[0],
    ]
    right = [corners[1], corners[2], twice(to_line(ub_last[0][:, 0:1]), to_line(g_next[0][:, 0:1]))]

    layer = lax.axis_index("layer")
    out[...] = jnp.zeros_like(out)
    for i, line in enumerate(left + right):
        out[8 + i : 9 + i, :] = line
    for i, values in enumerate((sum_zz[...], zb, bb, bbb)):
        out[pl.ds(2 * i + layer, 1), :] = jnp.sum(values, axis=0, keepdims=True)


def corner_kernel(others, mine, theirs, out):
    place, count, layer = lax.axis_index("col"), lax.axis_size("col"), lax.axis_index("layer")
    is_left = place % 2 == (1 if others else 0)
    here, there = mine[...], theirs[...]
    left, right = jnp.where(is_left, here, there), jnp.where(is_left, there, here)
    line = 2.0 * (left[8:9] * right[11:12] + left[9:10] * right[12:13] + left[10:11] * right[13:14])
    added = jnp.where(iota((8, LANES), 0) == 6 + layer, line, 0.0)
    if others:
        out[...] = here
        out[0:8] = here[0:8] + jnp.where(is_left & (place < count - 1), added, 0.0)
    else:
        out[...] = here[0:8] + there[0:8] + added


def ready_kernel(source, prof, factors, image, add_low, add_high, _, base, kept, sent):
    layer = lax.axis_index("layer")
    half, rows, width = source.shape[1:]
    count = 2 * half
    mine, theirs = factors[layer], factors[1 - layer]
    row = iota((rows, LANES), 0)

    def store(ref, where, scale, k):
        scale, plane = tiles_of(scale), tiles_of(image[k])
        for i, q in enumerate(plane):
            q = q + jnp.where(row == 0, add_low[pl.ds(i * count + k, 1), :], 0.0)
            q = q + jnp.where(row == rows - 1, add_high[pl.ds(i * count + k, 1), :], 0.0)
            ref[where, :, i * LANES : (i + 1) * LANES] = scale[i] * q

    def level(k):
        return jnp.broadcast_to(prof[pl.ds(k, 1), 0:1], (rows, width))

    def step(at, _):
        here, there = layer * half + at, (1 - layer) * half + at
        _, scale = gains(level(there) * mine)
        store(sent, at, scale, there)
        _, scale = gains(level(here) * mine)
        store(kept, at, scale, here)
        base[layer, at] = scale * (source_scale * source[layer, at])
        _, scale = gains(level(here) * theirs)
        base[1 - layer, at] = scale * (source_scale * source[1 - layer, at])
        return 0

    lax.fori_loop(0, half, step, 0, unroll=4)


def final_kernel(base, kept, received, sums, out, filled, left):
    layer = lax.axis_index("layer")
    half = base.shape[1]
    size = half // PIECES
    values = jnp.sum(sums[...], axis=1, keepdims=True)
    zz, zb, bb, bbb = (values[2 * i : 2 * i + 2] for i in range(4))
    delta = zz - zb
    alpha = zz / delta
    rest = -zb / delta
    beta = (zz * bb - zb * zb) / (delta * delta)
    gamma = zz * beta
    delta_next = gamma - (rest * rest * zb + 2.0 * alpha * rest * bb + alpha * alpha * bbb)
    alpha_next = gamma / (delta_next - beta * gamma / alpha)
    first, second = alpha + alpha_next * (rest + beta), alpha_next * alpha
    mine = iota((2, 1), 0) == layer
    copies = []
    for which, chosen, image in ((layer, mine, kept), (1 - layer, jnp.logical_not(mine), received)):
        a, b = (
            jnp.broadcast_to(jnp.sum(jnp.where(chosen, factor, 0.0), axis=0, keepdims=True), base.shape[2:])
            for factor in (first, second)
        )
        for piece in range(PIECES):
            for k in range(piece * size, (piece + 1) * size):
                filled[which, k] = a * base[which, k] + b * image[k]
            part = pl.ds(piece * size, size)
            copy = pltpu.make_async_copy(filled.at[which, part], out.at[which, part], left.at[len(copies)])
            copy.start()
            copies.append(copy)
    for copy in copies:
        copy.wait()


VMEM = pl.BlockSpec(memory_space=pltpu.VMEM)
SMEM = pl.BlockSpec(memory_space=pltpu.SMEM)


def call(kernel, out_shape, args, scalars=(), scratch=(), aliases=None, cost=0):
    return pl.pallas_call(
        kernel,
        out_shape=[jax.ShapeDtypeStruct(shape, jnp.float32) for shape in out_shape],
        in_specs=[SMEM if i in scalars else VMEM for i in range(len(args))],
        out_specs=[VMEM] * len(out_shape),
        scratch_shapes=[pltpu.VMEM(shape, jnp.float32) for shape in scratch],
        input_output_aliases=aliases or {},
        compiler_params=pltpu.CompilerParams(vmem_limit_bytes=GRANT),
        cost_estimate=pl.CostEstimate(flops=cost, bytes_accessed=cost, transcendentals=0) if cost else None,
    )(*args)


def solve(source, profile, column, terrain_height_error):
    copies, half, rows, width = source.shape
    count, tiles = 2 * half, width // LANES
    assert lax.axis_size("layer") == copies == 2 and count < LANES // 2 and width % LANES == 0
    assert count % 8 == 0 and rows % 8 == 0 and rows > 2 and half % CHUNKS == half % PIECES == 0
    swap = [(0, 1), (1, 0)]
    other = lax.ppermute(source, "layer", swap)
    profile_other = lax.ppermute(profile, "layer", swap)
    nr = tiles * count
    block, row, pack = (count, rows, width), (nr, LANES), (rows, LANES)
    strip = (-(-(2 * nr + tiles) // 8) * 8, LANES)
    shapes = [block, block, strip, strip, pack, pack, (count, LANES), (8, LANES)]
    lines = (-(-half // 8) * 8, LANES)
    factors = column * (1.0 + 0.002 * terrain_height_error.astype(jnp.float32))
    own = pl.pallas_call(
        own_kernel,
        out_shape=[jax.ShapeDtypeStruct(shape, jnp.float32) for shape in shapes],
        in_specs=[pl.BlockSpec(memory_space=pltpu.HBM), VMEM, VMEM],
        out_specs=[VMEM] * len(shapes),
        scratch_shapes=[
            pltpu.VMEM((half, rows, width), jnp.float32),
            pltpu.VMEM(lines, jnp.float32),
            pltpu.SemaphoreType.DMA((CHUNKS,)),
        ],
        compiler_params=pltpu.CompilerParams(vmem_limit_bytes=OWN_GRANT),
        name="own",
    )
    begun = own(source, profile, factors)
    weighted, gain, strip_low, strip_high, cols_low, cols_high, prof, sum_zz = call(
        other_kernel,
        shapes,
        (other, profile_other, factors, *begun),
        scratch=(lines,),
        aliases={3 + i: i for i in range(8)},
    )
    even = lax.axis_index("col") % 2 == 0
    pair_cols, other_cols = exchanged(
        jnp.where(even, cols_high, cols_low), jnp.where(even, cols_low, cols_high), "col"
    )
    image, g_low, g_high = call(image_kernel, [block, row, row], (weighted, gain))
    even = lax.axis_index("tile") % 2 == 0
    pair_strip, other_strip = exchanged(
        jnp.where(even, strip_high, strip_low), jnp.where(even, strip_low, strip_high), "tile"
    )
    image, q_low, q_high, k_low, k_high, packed, sum_rest = call(
        inner_kernel,
        [block, row, row, row, row, pack, (3, 8, LANES)],
        (image, weighted, gain, pair_cols, other_cols),
        scratch=(block,),
    )
    sums, add_low, add_high = call(
        finish_kernel,
        [(16, LANES), row, row],
        (
            pair_strip,
            other_strip,
            strip_low,
            strip_high,
            q_low,
            q_high,
            g_low,
            g_high,
            k_low,
            k_high,
            packed,
            cols_high,
            pair_cols,
            other_cols,
            prof,
            sum_zz,
            sum_rest,
        ),
    )
    part = (half, rows, width)
    cols = lax.axis_size("col")
    if cols > 2:
        _, theirs = exchanged(sums, sums, "col")
        (sums,) = call(functools.partial(corner_kernel, True), [(16, LANES)], (sums, theirs))
    if cols > 1:
        sizes = {"col": cols}
        theirs = flipped(sums, sizes, ("col",), (1,))
        (sums,) = call(functools.partial(corner_kernel, False), [(8, LANES)], (sums, theirs))
    else:
        sums = sums[0:8]
    later = total(sums)
    base, kept, sent = call(
        ready_kernel, [source.shape, part, part], (source, prof, factors, image, add_low, add_high, sums)
    )
    received = lax.ppermute(sent, "layer", swap)
    sums = later(sums)
    return pl.pallas_call(
        final_kernel,
        out_shape=jax.ShapeDtypeStruct(source.shape, jnp.float32),
        in_specs=[VMEM] * 4,
        out_specs=pl.BlockSpec(memory_space=pltpu.HBM),
        scratch_shapes=[pltpu.VMEM(source.shape, jnp.float32), pltpu.SemaphoreType.DMA((2 * PIECES,))],
        compiler_params=pltpu.CompilerParams(vmem_limit_bytes=GRANT),
        name="final",
    )(base, kept, received, sums)


def solution(mesh):
    placed = (
        P("group", "layer", "tile", "col"),
        P("layer"),
        P(("group", "tile"), "col"),
        P("group", "tile", "col"),
    )
    return jax.shard_map(
        solve,
        mesh=mesh,
        in_specs=placed,
        out_specs=P("group", "layer", "tile", "col"),
        check_vma=False,
    )
```

```python
import functools

import jax
import jax.numpy as jnp
from jax import lax
from jax.experimental import pallas as pl
from jax.experimental.pallas import tpu as pltpu
from jax.sharding import PartitionSpec as P


weight_vert = 2.0
weight_cross = 0.3
gain_bound = 1.6
total_weight = 10.4
diag_shift = 0.5
source_scale = 8.0

LANES = 128
GRANT = 8 << 20
OWN_GRANT = 53_750_000
CHUNKS = 2
PIECES = 4


def line_pairs(count, first):
    pairs = []
    for low in range(first, count - 1, 2):
        pairs += [(low, low + 1), (low + 1, low)]
    return pairs


def exchanged(for_pairs, for_others, axis):
    count, layers = lax.axis_size(axis), lax.axis_size("layer")
    received = []
    for first, values in ((0, for_pairs), (1, for_others)):
        partner = dict(line_pairs(count, first))
        if not partner:
            received.append(jnp.zeros_like(values))
            continue
        pairs = []
        for place in range(count):
            for layer in range(layers):
                target = (partner[place], layer) if place in partner else (place, layers - 1 - layer)
                pairs.append((place * layers + layer, target[0] * layers + target[1]))
        received.append(lax.ppermute(values, (axis, "layer"), pairs))
    return received


def halves(first, second, axis):
    place, count = lax.axis_index(axis), lax.axis_size(axis)
    even = place % 2 == 0
    low = jnp.where(place > 0, jnp.where(even, second, first), 0.0)
    high = jnp.where(place < count - 1, jnp.where(even, first, second), 0.0)
    return low, high


def flipped(values, sizes, axes, bits):
    shape = [sizes[axis] for axis in axes]
    pairs = []
    for flat in range(functools.reduce(lambda a, b: a * b, shape, 1)):
        place, rest = [], flat
        for size in reversed(shape):
            place.insert(0, rest % size)
            rest //= size
        target = 0
        for where, size, bit in zip(place, shape, bits):
            target = target * size + (where ^ bit)
        pairs.append((flat, target))
    return lax.ppermute(values, axes, pairs)


def total(values):
    sizes = {axis: lax.axis_size(axis) for axis in ("layer", "col", "tile")}
    assert all(size & (size - 1) == 0 for size in sizes.values())
    both = sizes["tile"] > 1
    first = flipped(values, sizes, ("layer",), (1,))
    if both:
        first = first + flipped(values, sizes, ("tile",), (1,))
        first = first + flipped(values, sizes, ("tile", "layer"), (1, 1))

    def later(values):
        values = values + first
        for axis, bit in (("tile", 2 if both else 1), ("col", 2)):
            while bit < sizes[axis]:
                values = values + flipped(values, sizes, (axis,), (bit,))
                bit *= 2
        return values

    return later


def tiles_of(plane):
    return [plane[:, at : at + LANES] for at in range(0, plane.shape[1], LANES)]


def iota(shape, axis):
    return lax.broadcasted_iota(jnp.int32, shape, axis)


def turned(values, by, axis):
    by %= values.shape[axis]
    return pltpu.roll(values, by, axis) if by else values


def sides(tiles):
    rows, lanes = tiles[0].shape
    row, lane = iota((rows, lanes), 0), iota((rows, lanes), 1)
    ahead = [turned(tile, -1, 1) for tile in tiles] + [0.0]
    behind = [0.0] + [turned(tile, 1, 1) for tile in tiles]
    out = []
    for i, tile in enumerate(tiles):
        below = jnp.where(row == rows - 1, 0.0, turned(tile, -1, 0))
        above = jnp.where(row == 0, 0.0, turned(tile, 1, 0))
        right = jnp.where(lane == lanes - 1, ahead[i + 1], ahead[i])
        left = jnp.where(lane == 0, behind[i], behind[i + 1])
        out.append((below + above) + (right + left))
    return out


def levels(tiles, side):
    return [weight_vert * tile + weight_cross * s for tile, s in zip(tiles, side)]


def gains(metric):
    scale = metric / (gain_bound * total_weight * metric + diag_shift)
    return metric * scale, scale


def folded(values):
    return functools.reduce(lambda a, b: a + b, [values[at : at + 8] for at in range(0, values.shape[0], 8)])


def dot(left, right):
    return functools.reduce(lambda a, b: a + b, [folded(a * b) for a, b in zip(left, right)])


def keep_rows(k, tiles, low, high, count):
    rows = tiles[0].shape[0]
    for i, tile in enumerate(tiles):
        if low is not None:
            low[pl.ds(i * count + k, 1), :] = tile[0:1]
        if high is not None:
            high[pl.ds(i * count + k, 1), :] = tile[rows - 1 : rows]


def weigh(k, forcing, level, columns, refs):
    weighted, gain, strip_low, strip_high, prof = refs
    count, tiles = weighted.shape[0], len(forcing)
    parts = []
    for i, (y, column) in enumerate(zip(forcing, columns)):
        g, _ = gains(level * column)
        u = g * y
        weighted[k, :, i * LANES : (i + 1) * LANES] = u
        gain[k, :, i * LANES : (i + 1) * LANES] = g
        strip_low[pl.ds((tiles + i) * count + k, 1), :] = u[1:2]
        parts.append(u)
    keep_rows(k, parts, strip_low, strip_high, count)
    prof[pl.ds(k, 1), :] = level
    return parts, dot(parts, forcing)


def level_rows(profile, rows):
    line = profile[...][None]
    square = (rows.shape[0], line.shape[1])
    column = jnp.sum(jnp.where(iota(square, 0) == iota(square, 1), line, 0.0), axis=1, keepdims=True)
    rows[...] = jnp.broadcast_to(column, rows.shape)


def weigh_planes(start, stop, unroll, base, read, levels_at, columns, carry, refs):
    lane = iota(columns[0].shape, 1)

    def step(at, carry):
        first, second, last, acc = carry
        k = base + at
        forcing = [source_scale * tile for tile in tiles_of(read(at))]
        parts, share = weigh(k, forcing, levels_at[pl.ds(at, 1), :], columns, refs)
        first = jnp.where(lane == k, pltpu.roll(parts[0], k, 1), first)
        at_second = k + LANES // 2
        second = jnp.where(lane == at_second, pltpu.roll(parts[0], at_second - 1, 1), second)
        last = jnp.where(lane == k, pltpu.roll(parts[-1], k + 1, 1), last)
        return first, second, last, acc + share

    return lax.fori_loop(start, stop, step, carry, unroll=unroll)


def own_kernel(
    held, profile, factors, weighted, gain, strip_low, strip_high, cols_low, cols_high, prof, sums, plane, levels_at, arrived
):
    layer = lax.axis_index("layer")
    half, rows, width = plane.shape
    count, tiles = 2 * half, width // LANES
    size = half // CHUNKS
    parts = [slice(i * size, (i + 1) * size) for i in range(CHUNKS)]
    copies = [pltpu.make_async_copy(held.at[layer, part], plane.at[part], arrived.at[i]) for i, part in enumerate(parts)]
    for copy in copies:
        copy.start()
    columns = tiles_of(factors[layer])
    level_rows(profile, levels_at)
    lane = iota((rows, LANES), 1)
    for i, tile in enumerate(columns):
        strip_low[2 * tiles * count + i : 2 * tiles * count + i + 1, :] = tile[0:1]
    zeros = jnp.zeros((rows, LANES), jnp.float32)
    edge = jnp.where(lane == LANES - 1, turned(columns[0], -1, 1), 0.0)
    carry = (edge, zeros, zeros, jnp.zeros((8, LANES), jnp.float32))
    refs = (weighted, gain, strip_low, strip_high, prof)
    for part, copy in zip(parts, copies):
        copy.wait()
        carry = weigh_planes(
            part.start, part.stop, size, layer * half, lambda at: plane[at], levels_at, columns, carry, refs
        )
    first, second, cols_high[...], sums[...] = carry
    cols_low[...] = first + second


def other_kernel(source, profile, factors, *refs):
    weighted, gain, strip_low, strip_high, cols_low, cols_high, prof, sums, levels_at = refs[8:]
    layer = lax.axis_index("layer")
    half = source.shape[1]
    columns = tiles_of(factors[layer])
    level_rows(profile, levels_at)
    zeros = jnp.zeros(columns[0].shape, jnp.float32)
    first, second, cols_high[...], sums[...] = weigh_planes(
        0,
        half,
        20,
        (1 - layer) * half,
        lambda at: source[layer, at],
        levels_at,
        columns,
        (refs[4][...], zeros, refs[5][...], refs[7][...]),
        (weighted, gain, strip_low, strip_high, prof),
    )
    cols_low[...] = first + second


def shifts(values, axis):
    size = values.shape[axis]
    place = iota(values.shape, axis)
    up = jnp.where(place == size - 1, 0.0, turned(values, -1, axis))
    down = jnp.where(place == 0, 0.0, turned(values, 1, axis))
    return up + down


def near(values, axis):
    return values + weight_cross * shifts(values, axis)


def swept(count, width, rows, plane, emit, carry):
    zero = [jnp.zeros((rows, LANES), jnp.float32) for _ in range(width // LANES)]

    def step(k, state):
        side_before, level_twice, level_before, carry = state
        tiles, carry = plane(k, carry)
        side = sides(tiles)
        level = levels(tiles, side)
        found = [s + a + b for s, a, b in zip(side_before, level_twice, level)]
        return side, level_before, level, emit(k - 1, found, carry)

    tiles, carry = plane(0, carry)
    side = sides(tiles)
    state = (side, zero, levels(tiles, side), carry)
    side, level_twice, _, carry = lax.fori_loop(1, count, step, state, unroll=13)
    return emit(count - 1, [s + a for s, a in zip(side, level_twice)], carry)


def put(ref, k, tiles):
    for i, tile in enumerate(tiles):
        ref[k, :, i * LANES : (i + 1) * LANES] = tile


def image_kernel(weighted, gain, image, g_low, g_high):
    count, rows, width = weighted.shape

    def plane(k, carry):
        return tiles_of(weighted[k]), carry

    def emit(k, found, carry):
        put(image, k, found)
        keep_rows(k, tiles_of(gain[k]), g_low, g_high, count)
        return carry

    swept(count, width, rows, plane, emit, 0)


def inner_kernel(begun, weighted, gain, pair_cols, other_cols, image, q_low, q_high, k_low, k_high, pack, sums, again):
    count, rows, width = weighted.shape
    lane = iota((rows, LANES), 1)
    low, high = halves(pair_cols[...], other_cols[...], "col")
    add_low = near(jnp.where(lane < count, low, 0.0), 1)
    add_high = near(jnp.where(lane < count, high, 0.0), 1)
    one = jnp.zeros((8, LANES), jnp.float32)

    def step(k, carry):
        packed, zb, bb = carry
        u, g, q = tiles_of(weighted[k]), tiles_of(gain[k]), tiles_of(begun[k])
        q[0] = q[0] + jnp.where(lane == 0, pltpu.roll(add_low, lax.rem(LANES - k, LANES), 1), 0.0)
        q[-1] = q[-1] + jnp.where(lane == LANES - 1, pltpu.roll(add_high, LANES - 1 - k, 1), 0.0)
        ub = [a * b for a, b in zip(g, q)]
        put(image, k, q)
        put(again, k, ub)
        keep_rows(k, q, q_low, q_high, count)
        packed = jnp.where(lane == k, pltpu.roll(ub[-1], k + 1, 1), packed)
        return packed, zb + dot(u, q), bb + dot(ub, q)

    def emit(k, found, bbb):
        keep_rows(k, found, k_low, k_high, count)
        return bbb + dot(tiles_of(again[k]), found)

    packed, zb, bb = lax.fori_loop(0, count, step, (jnp.zeros((rows, LANES), jnp.float32), one, one), unroll=8)
    bbb = swept(count, width, rows, lambda k, carry: (tiles_of(again[k]), carry), emit, one)
    pack[...] = packed
    sums[0], sums[1], sums[2] = zb, bb, bbb


def along(tiles, left, right):
    lane = iota(tiles[0].shape, 1)
    ahead = [turned(tile, -1, 1) for tile in tiles] + [right]
    behind = [left] + [turned(tile, 1, 1) for tile in tiles]
    return [
        jnp.where(lane == LANES - 1, ahead[i + 1], ahead[i]) + jnp.where(lane == 0, behind[i], behind[i + 1])
        for i in range(len(tiles))
    ]


def finish_kernel(
    pair_strip,
    other_strip,
    strip_low,
    strip_high,
    q_low,
    q_high,
    g_low,
    g_high,
    k_low,
    k_high,
    pack,
    last,
    pair_cols,
    other_cols,
    prof,
    sum_zz,
    sum_rest,
    out,
    add_low,
    add_high,
):
    count = prof.shape[0]
    nr = q_low.shape[0]
    tiles = nr // count
    rows = pack.shape[0]
    low, high = halves(pair_strip[...], other_strip[...], "tile")
    _, high_cols = halves(pair_cols[...], other_cols[...], "col")

    def blocks(values, start=0):
        return [values[start + i * count : start + (i + 1) * count] for i in range(tiles)]

    shape = (count, LANES)
    diagonal = iota(shape, 0) == iota(shape, 1)

    def to_line(column):
        return jnp.sum(jnp.where(diagonal, column, 0.0), axis=0, keepdims=True)

    def total(left, right):
        return dot(left, right)

    zb, bb, bbb = sum_rest[0], sum_rest[1], sum_rest[2]
    outer = []
    for halo, u, q, g, ka, add in (
        (low, strip_low, q_low, g_low, k_low, add_low),
        (high, strip_high, q_high, g_high, k_high, add_high),
    ):
        h = [near(block, 0) for block in blocks(halo)]
        for i, block in enumerate(h):
            add[i * count : (i + 1) * count, :] = block
        u, q, g, ka = blocks(u[...]), blocks(q[...]), blocks(g[...]), blocks(ka[...])
        e = [a * b for a, b in zip(g, h)]
        side = along(e, 0.0, 0.0)
        ke = [s + shifts(weight_vert * a + weight_cross * s, 0) for a, s in zip(e, side)]
        zb = zb + total(u, h)
        bb = bb + total(e, [2.0 * a + b for a, b in zip(q, h)])
        bbb = bbb + total(e, [2.0 * a + b for a, b in zip(ka, ke)])
        outer.append((u, e, [a * b + c for a, b, c in zip(g, q, e)]))
    (_, e_low, ub_first), (u_last, e_high, ub_last) = outer
    corners = [to_line(high[(tiles - 1) * count : tiles * count][:, LANES - 1 :])]
    corners += [to_line(values[0:count][:, 0:1]) for values in (high, low)]

    u_next, u_after = blocks(high), blocks(high, nr)
    side = along(u_next, 0.0, 0.0)
    side = [s + a + b for s, a, b in zip(side, u_last, u_after)]
    q_next = [s + shifts(weight_vert * a + weight_cross * s, 0) for a, s in zip(u_next, side)]
    level = prof[...]
    g_next = [gains(level * high[2 * nr + i : 2 * nr + i + 1])[0] for i in range(tiles)]
    for i in range(tiles):
        bbb = bbb + 2.0 * folded(ub_last[i] * near(g_next[i] * q_next[i], 0))

    lane, row = iota((rows, LANES), 1), iota((rows, LANES), 0)
    held = lane < count
    u_next = jnp.where(held, high_cols, 0.0)
    up = jnp.where(row == 0, 0.0, turned(u_next, 1, 0))
    down = jnp.where(row == rows - 1, 0.0, turned(u_next, -1, 0))
    side = last[...] + jnp.where(held, turned(high_cols, LANES // 2, 1), 0.0) + up + down
    q_next = side + shifts(weight_vert * u_next + weight_cross * side, 1)
    g, _ = gains(to_line(level) * high_cols[:, LANES - 1 :])
    ub = pack[...]
    ub = ub + jnp.where(row == 0, to_line(e_low[-1][:, LANES - 1 :]), 0.0)
    ub = ub + jnp.where(row == rows - 1, to_line(e_high[-1][:, LANES - 1 :]), 0.0)
    bbb = bbb + 2.0 * folded(ub * near(g * q_next, 1))

    def twice(value, gain):
        value, gain = jnp.broadcast_to(value, (8, LANES)), jnp.broadcast_to(gain, (8, LANES))
        return near(gain * near(value, 1), 1)[0:1]

    last_line, first_line = (to_line(ub[-1][:, LANES - 1 :]) for ub in (ub_last, ub_first))
    left = [
        twice(last_line, to_line(g_next[-1][:, LANES - 1 :]) + g[rows - 1 : rows]),
        twice(first_line, g[0:1]),
        corners[0],
    ]
    right = [corners[1], corners[2], twice(to_line(ub_last[0][:, 0:1]), to_line(g_next[0][:, 0:1]))]

    layer = lax.axis_index("layer")
    out[...] = jnp.zeros_like(out)
    for i, line in enumerate(left + right):
        out[8 + i : 9 + i, :] = line
    for i, values in enumerate((sum_zz[...], zb, bb, bbb)):
        out[pl.ds(2 * i + layer, 1), :] = jnp.sum(values, axis=0, keepdims=True)


def corner_kernel(others, mine, theirs, out):
    place, count, layer = lax.axis_index("col"), lax.axis_size("col"), lax.axis_index("layer")
    is_left = place % 2 == (1 if others else 0)
    here, there = mine[...], theirs[...]
    left, right = jnp.where(is_left, here, there), jnp.where(is_left, there, here)
    line = 2.0 * (left[8:9] * right[11:12] + left[9:10] * right[12:13] + left[10:11] * right[13:14])
    added = jnp.where(iota((8, LANES), 0) == 6 + layer, line, 0.0)
    if others:
        out[...] = here
        out[0:8] = here[0:8] + jnp.where(is_left & (place < count - 1), added, 0.0)
    else:
        out[...] = here[0:8] + there[0:8] + added


def ready_kernel(source, prof, factors, image, add_low, add_high, _, base, kept, sent):
    layer = lax.axis_index("layer")
    half, rows, width = source.shape[1:]
    count = 2 * half
    mine, theirs = factors[layer], factors[1 - layer]
    row = iota((rows, LANES), 0)

    def store(ref, where, scale, k):
        scale, plane = tiles_of(scale), tiles_of(image[k])
        for i, q in enumerate(plane):
            q = q + jnp.where(row == 0, add_low[pl.ds(i * count + k, 1), :], 0.0)
            q = q + jnp.where(row == rows - 1, add_high[pl.ds(i * count + k, 1), :], 0.0)
            ref[where, :, i * LANES : (i + 1) * LANES] = scale[i] * q

    def level(k):
        return jnp.broadcast_to(prof[pl.ds(k, 1), 0:1], (rows, width))

    def step(at, _):
        here, there = layer * half + at, (1 - layer) * half + at
        _, scale = gains(level(there) * mine)
        store(sent, at, scale, there)
        _, scale = gains(level(here) * mine)
        store(kept, at, scale, here)
        base[layer, at] = scale * (source_scale * source[layer, at])
        _, scale = gains(level(here) * theirs)
        base[1 - layer, at] = scale * (source_scale * source[1 - layer, at])
        return 0

    lax.fori_loop(0, half, step, 0, unroll=4)


def final_kernel(base, kept, received, sums, out, filled, left):
    layer = lax.axis_index("layer")
    half = base.shape[1]
    size = half // PIECES
    values = jnp.sum(sums[...], axis=1, keepdims=True)
    zz = values[0:2]
    zb, bb, bbb = (values[2 * i : 2 * i + 2] / zz for i in range(1, 4))
    delta = 1.0 - zb
    alpha = 1.0 / delta
    rest = -zb * alpha
    beta = (bb - zb * zb) * (alpha * alpha)
    delta_next = beta - (rest * rest * zb + 2.0 * alpha * rest * bb + alpha * alpha * bbb)
    alpha_next = beta / (delta_next - beta * beta * delta)
    first, second = alpha + alpha_next * (rest + beta), alpha_next * alpha
    mine = iota((2, 1), 0) == layer
    copies = []
    for which, chosen, image in ((layer, mine, kept), (1 - layer, jnp.logical_not(mine), received)):
        a, b = (
            jnp.broadcast_to(jnp.sum(jnp.where(chosen, factor, 0.0), axis=0, keepdims=True), base.shape[2:])
            for factor in (first, second)
        )
        for piece in range(PIECES):
            for k in range(piece * size, (piece + 1) * size):
                filled[which, k] = a * base[which, k] + b * image[k]
            part = pl.ds(piece * size, size)
            copy = pltpu.make_async_copy(filled.at[which, part], out.at[which, part], left.at[len(copies)])
            copy.start()
            copies.append(copy)
    for copy in copies:
        copy.wait()


VMEM = pl.BlockSpec(memory_space=pltpu.VMEM)
SMEM = pl.BlockSpec(memory_space=pltpu.SMEM)


def call(kernel, out_shape, args, scalars=(), scratch=(), aliases=None, cost=0):
    return pl.pallas_call(
        kernel,
        out_shape=[jax.ShapeDtypeStruct(shape, jnp.float32) for shape in out_shape],
        in_specs=[SMEM if i in scalars else VMEM for i in range(len(args))],
        out_specs=[VMEM] * len(out_shape),
        scratch_shapes=[pltpu.VMEM(shape, jnp.float32) for shape in scratch],
        input_output_aliases=aliases or {},
        compiler_params=pltpu.CompilerParams(vmem_limit_bytes=GRANT),
        cost_estimate=pl.CostEstimate(flops=cost, bytes_accessed=cost, transcendentals=0) if cost else None,
    )(*args)


def solve(source, profile, column, terrain_height_error):
    copies, half, rows, width = source.shape
    count, tiles = 2 * half, width // LANES
    assert lax.axis_size("layer") == copies == 2 and count < LANES // 2 and width % LANES == 0
    assert count % 8 == 0 and rows % 8 == 0 and rows > 2 and half % CHUNKS == half % PIECES == 0
    swap = [(0, 1), (1, 0)]
    other = lax.ppermute(source, "layer", swap)
    profile_other = lax.ppermute(profile, "layer", swap)
    nr = tiles * count
    block, row, pack = (count, rows, width), (nr, LANES), (rows, LANES)
    strip = (-(-(2 * nr + tiles) // 8) * 8, LANES)
    shapes = [block, block, strip, strip, pack, pack, (count, LANES), (8, LANES)]
    lines = (-(-half // 8) * 8, LANES)
    factors = column * (1.0 + 0.002 * terrain_height_error.astype(jnp.float32))
    own = pl.pallas_call(
        own_kernel,
        out_shape=[jax.ShapeDtypeStruct(shape, jnp.float32) for shape in shapes],
        in_specs=[pl.BlockSpec(memory_space=pltpu.HBM), VMEM, VMEM],
        out_specs=[VMEM] * len(shapes),
        scratch_shapes=[
            pltpu.VMEM((half, rows, width), jnp.float32),
            pltpu.VMEM(lines, jnp.float32),
            pltpu.SemaphoreType.DMA((CHUNKS,)),
        ],
        compiler_params=pltpu.CompilerParams(vmem_limit_bytes=OWN_GRANT),
        name="own",
    )
    begun = own(source, profile, factors)
    weighted, gain, strip_low, strip_high, cols_low, cols_high, prof, sum_zz = call(
        other_kernel,
        shapes,
        (other, profile_other, factors, *begun),
        scratch=(lines,),
        aliases={3 + i: i for i in range(8)},
    )
    even = lax.axis_index("col") % 2 == 0
    pair_cols, other_cols = exchanged(
        jnp.where(even, cols_high, cols_low), jnp.where(even, cols_low, cols_high), "col"
    )
    image, g_low, g_high = call(image_kernel, [block, row, row], (weighted, gain))
    even = lax.axis_index("tile") % 2 == 0
    pair_strip, other_strip = exchanged(
        jnp.where(even, strip_high, strip_low), jnp.where(even, strip_low, strip_high), "tile"
    )
    image, q_low, q_high, k_low, k_high, packed, sum_rest = call(
        inner_kernel,
        [block, row, row, row, row, pack, (3, 8, LANES)],
        (image, weighted, gain, pair_cols, other_cols),
        scratch=(block,),
    )
    sums, add_low, add_high = call(
        finish_kernel,
        [(16, LANES), row, row],
        (
            pair_strip,
            other_strip,
            strip_low,
            strip_high,
            q_low,
            q_high,
            g_low,
            g_high,
            k_low,
            k_high,
            packed,
            cols_high,
            pair_cols,
            other_cols,
            prof,
            sum_zz,
            sum_rest,
        ),
    )
    part = (half, rows, width)
    cols = lax.axis_size("col")
    if cols > 2:
        _, theirs = exchanged(sums, sums, "col")
        (sums,) = call(functools.partial(corner_kernel, True), [(16, LANES)], (sums, theirs))
    if cols > 1:
        sizes = {"col": cols}
        theirs = flipped(sums, sizes, ("col",), (1,))
        (sums,) = call(functools.partial(corner_kernel, False), [(8, LANES)], (sums, theirs))
    else:
        sums = sums[0:8]
    later = total(sums)
    base, kept, sent = call(
        ready_kernel, [source.shape, part, part], (source, prof, factors, image, add_low, add_high, sums)
    )
    received = lax.ppermute(sent, "layer", swap)
    sums = later(sums)
    return pl.pallas_call(
        final_kernel,
        out_shape=jax.ShapeDtypeStruct(source.shape, jnp.float32),
        in_specs=[VMEM] * 4,
        out_specs=pl.BlockSpec(memory_space=pltpu.HBM),
        scratch_shapes=[pltpu.VMEM(source.shape, jnp.float32), pltpu.SemaphoreType.DMA((2 * PIECES,))],
        compiler_params=pltpu.CompilerParams(vmem_limit_bytes=GRANT),
        name="final",
    )(base, kept, received, sums)


def solution(mesh):
    placed = (
        P("group", "layer", "tile", "col"),
        P("layer"),
        P(("group", "tile"), "col"),
        P("group", "tile", "col"),
    )
    return jax.shard_map(
        solve,
        mesh=mesh,
        in_specs=placed,
        out_specs=P("group", "layer", "tile", "col"),
        check_vma=False,
    )
```
